32 devices in a mesh: comp: 2 (over y), tile: 16 (over z, x, core).
Axes of the slice: x: 2, y: 2, z: 4, core: 2. Of those that a mesh axis runs over, the one named last changes fastest.
Arguments:
- air_winds_heights: float32 [3, 16, 256, 2048], P(None, None, 'tile', 'comp'), may hold values from -6 to 6
- exchange_coefficient_air: float32 [256, 2048], P('tile', 'comp'), may hold values from 0.5 to 2
- air_seen_warmness: float32 [256, 2048], P('tile', 'comp'), may hold values from 1 to 3
- marine_flow_vectors: float32 [2, 10, 128, 1024], P(None, None, 'tile', 'comp'), may hold values from -6 to 6
- marine_warmness: float32 [128, 1024], P('tile', 'comp'), may hold values from -6 to 6
- water_indicator: int32 [128, 1024], P('tile', 'comp'), may hold values 0 or 1
- partner_air_tiles: int32 [1024, 4], P(('comp', 'tile')), may hold values from 0 to 2047, as said below
- partner_tally_each_tile: int32 [1024], P(('comp', 'tile')), may hold values from 2 to 4, as said below
- partner_overlay_shares: bfloat16 [1024, 4, 128, 128], P(('comp', 'tile')), may hold values from 0.0009994507 to 1
Outputs:
- atmosphere_next: float32 [3, 16, 256, 2048], P(None, None, 'tile', 'comp')
- advanced_flows: float32 [2, 10, 128, 1024], P(None, None, 'tile', 'comp')
- advanced_warmness: float32 [128, 1024], P('tile', 'comp')
The draws below stay inside these ranges and needn't reach their ends.
Inputs may be any that keep to these rules, and one draw needn't show every extreme that they name: `partner_air_tiles`: every entry names an atmosphere block of the ocean block's own longitude half; for ocean block g with t = (g // 32) % 16 it lies from t * 128 - 8 to (t + 1) * 128 + 7, cut to the grid's blocks, and both ends of that range are named for every tile. `partner_tally_each_tile`: the first ocean block of every tile has all 4 slots live.
All inputs are finite; a program needn't handle non-finite values. No bound on the sum of `water_indicator` on one device may be relied on, other than what follows from the above.
Results may differ from the reference program's by a relative error of at most 0.0003.
Values sent between devices are 32-bit elements; how exact they have to be, the bound alone decides.
A program may use at most 128 MiB of HBM per device.

```python
import math
import jax
import jax.numpy as jnp
from jax import lax

LEV_A = 16
MARINE_DEPTHS = 10
ALAT = 16
ALON = 1024
BLOCK = 128
NOV = 4
HB = 8
OLAT = 8
OLON = 512
NAB = 128
NOB = 32
TILES = 16
AIR_GRID_HEIGHT = 256
AIR_GRID_WIDTH = 2048
MARINE_HEIGHT = 128
MARINE_WIDTH = 1024
NOB_ALL = 1024
N_COMP = 2
N_TILE = 16


def draw_partner_air_tiles(key, part):
    block_ids = jnp.arange(NOB_ALL, dtype=jnp.int32)
    tile_ids = block_ids // NOB % TILES
    local_ids = block_ids % NOB
    low_end = tile_ids * NAB - HB
    span_width = NAB + 2 * HB
    offsets = jax.random.randint(key, (NOB_ALL, NOV), 0, span_width, dtype=jnp.int32)
    picked = low_end[:, None] + offsets
    first_slot = jnp.where(local_ids == 0, low_end, picked[:, 0])
    second_slot = jnp.where(local_ids == NOB - 1, low_end + span_width - 1, picked[:, 1])
    picked = jnp.concatenate([first_slot[:, None], second_slot[:, None], picked[:, 2:]], axis=1)
    return jnp.clip(picked, 0, NAB * TILES - 1).astype(jnp.int32)


def draw_partner_tally_each_tile(key, part):
    block_ids = jnp.arange(NOB_ALL, dtype=jnp.int32)
    drawn = jax.random.randint(key, (NOB_ALL,), 2, NOV + 1, dtype=jnp.int32)
    return jnp.where(block_ids % NOB == 0, NOV, drawn).astype(jnp.int32)


def place_ends(values, key, low, largest):
    extent = values.shape
    place = [jax.random.randint(jax.random.fold_in(key, axis), (), 0, extent[axis]) for axis in range(len(extent))]
    values = values.at[tuple(place)].set(low)
    longest = extent.index(max(extent))
    place[longest] = (place[longest] + 1) % extent[longest]
    return values.at[tuple(place)].set(largest)


def shard_levels(own_key, dims, pieces, low, top_value):
    def one(dim, parts):
        steps = jax.random.uniform(jax.random.fold_in(jax.random.fold_in(own_key, 6), dim), (parts,), jnp.float32, low / len(pieces), top_value / len(pieces))
        return jnp.repeat(jnp.exp(steps), dims[dim] // parts).reshape((-1,) + (1,) * (len(dims) - dim - 1))

    factor_of = one(*pieces[0])
    for cut in pieces[1:]:
        factor_of = factor_of * one(*cut)
    return factor_of


def normal_values(own_key, extent, deviation, most, pieces=(), kind=jnp.bfloat16):
    values = jax.random.normal(own_key, extent, jnp.float32) * deviation
    if len(pieces) > 0:
        values = shard_levels(own_key, extent, pieces, -0.22, 0.18) * values
    return jnp.clip(values, min=-most, max=most).astype(kind)


def setup_inputs(seed: int = 0) -> dict:
    arg_keys = jax.random.split(jax.random.key(seed), 10)
    return {
        "air_winds_heights": normal_values(arg_keys[0], (3, LEV_A, AIR_GRID_HEIGHT, AIR_GRID_WIDTH), 1.0, 6.0, ((2, 16), (3, 2)), jnp.float32),
        "exchange_coefficient_air": jnp.clip(jnp.exp(math.log(2.0) - 1.3862944 * jax.random.uniform(arg_keys[1], (AIR_GRID_HEIGHT, AIR_GRID_WIDTH), jnp.float32) ** shard_levels(arg_keys[1], (AIR_GRID_HEIGHT, AIR_GRID_WIDTH), ((0, 16), (1, 2)), -0.2, 0.2)), 0.5, 2.0),
        "air_seen_warmness": jnp.clip(1.0 + 2.0 * jax.random.uniform(arg_keys[2], (AIR_GRID_HEIGHT, AIR_GRID_WIDTH), jnp.float32) ** shard_levels(arg_keys[2], (AIR_GRID_HEIGHT, AIR_GRID_WIDTH), ((0, 16), (1, 2)), -0.2, 0.2), 1.0, 3.0),
        "marine_flow_vectors": normal_values(arg_keys[3], (2, MARINE_DEPTHS, MARINE_HEIGHT, MARINE_WIDTH), 1.0, 6.0, ((2, 16), (3, 2)), jnp.float32),
        "marine_warmness": normal_values(arg_keys[4], (MARINE_HEIGHT, MARINE_WIDTH), 1.0, 6.0, ((0, 16), (1, 2)), jnp.float32),
        "water_indicator": place_ends((jax.random.randint(arg_keys[5], (MARINE_HEIGHT, MARINE_WIDTH), 0, 10) < 7).astype(jnp.int32), jax.random.fold_in(arg_keys[5], 1), 0, 1),
        "partner_air_tiles": draw_partner_air_tiles(jax.random.fold_in(arg_keys[9], 71), 0),
        "partner_tally_each_tile": draw_partner_tally_each_tile(jax.random.fold_in(arg_keys[9], 71), 0),
        "partner_overlay_shares": jnp.clip(jnp.exp(math.log(1.0) - 6.9083047 * jax.random.uniform(arg_keys[8], (NOB_ALL, NOV, BLOCK, BLOCK), jnp.float32) ** shard_levels(arg_keys[8], (NOB_ALL, NOV, BLOCK, BLOCK), ((0, 32),), -0.2, 0.2)), 0.0009994507, 1.0).astype(jnp.bfloat16),
    }


step_atmos = 0.2
coriolis_atmos = 0.3
visc_atmos = 1.0
mixing_atmos = 0.5
gust_square = 0.25
step_ocean = 0.2
coriolis_ocean = 0.3
visc_ocean = 1.0
mixing_ocean = 0.5
heat_gain = 1.0
diffuse_ocean = 0.5

def vertical(joined_quantities):
    upper = jnp.concatenate([joined_quantities[1:], joined_quantities[-1:]], axis=0)
    lower = jnp.concatenate([joined_quantities[:1], joined_quantities[:-1]], axis=0)
    return upper - 2.0 * joined_quantities + lower

def stencil(bordered_argument):
    centre = bordered_argument[..., 1:-1, 1:-1]
    below_row = bordered_argument[..., :-2, 1:-1]
    above_row = bordered_argument[..., 2:, 1:-1]
    left_col = bordered_argument[..., 1:-1, :-2]
    right_col = bordered_argument[..., 1:-1, 2:]
    laplace = above_row + below_row + left_col + right_col - 4.0 * centre
    east_grad = 0.5 * (right_col - left_col)
    north_grad = 0.5 * (above_row - below_row)
    return (centre, laplace, east_grad, north_grad)

def advance(bordered_argument):
    centre, laplace, east_grad, north_grad = stencil(bordered_argument)
    zonal_flow, meridional_flow, depth_anomaly_sheet = (centre[0], centre[1], centre[2])
    new_east = zonal_flow + step_atmos * (coriolis_atmos * meridional_flow - east_grad[2] + visc_atmos * laplace[0] + mixing_atmos * vertical(zonal_flow))
    new_north = meridional_flow + step_atmos * (-coriolis_atmos * zonal_flow - north_grad[2] + visc_atmos * laplace[1] + mixing_atmos * vertical(meridional_flow))
    new_thick = depth_anomaly_sheet + step_atmos * (-(east_grad[0] + north_grad[1]) + visc_atmos * laplace[2] + mixing_atmos * vertical(depth_anomaly_sheet))
    return jnp.stack([new_east, new_north, new_thick])

def uppermost_sheet(joined_quantities, exchange_coefficient_air, air_seen_warmness):
    zonal_flow = joined_quantities[0, 0]
    meridional_flow = joined_quantities[1, 0]
    depth_anomaly_sheet = joined_quantities[2, 0]
    wind_speed = jnp.sqrt(zonal_flow * zonal_flow + meridional_flow * meridional_flow + gust_square)
    multiplier_coefficient = exchange_coefficient_air * wind_speed
    return jnp.stack([multiplier_coefficient * zonal_flow, multiplier_coefficient * meridional_flow, multiplier_coefficient * (air_seen_warmness - depth_anomaly_sheet)])

def remap_blocks(chosen, counts, weights):
    live_slots = (jnp.arange(weights.shape[1])[None, :] < counts[:, None]).astype(jnp.float32)
    masked = weights.astype(jnp.float32) * live_slots[:, :, None, None]
    numerator = jnp.einsum('fjsa,jsao->fjo', chosen, masked, precision=lax.Precision.HIGHEST)
    denominator = lax.optimization_barrier(jnp.sum(masked, axis=(1, 2)))
    return numerator / denominator[None]

def marine_drift_advance(bordered_argument, regridded_exchanges, sea_mask):
    centre, laplace, east_grad, north_grad = stencil(bordered_argument)
    levels = (centre.shape[0] - 1) // 2
    zonal_flow = centre[:levels]
    meridional_flow = centre[levels:2 * levels]
    warmth = centre[2 * levels]
    blank_levels = jnp.zeros_like(zonal_flow[1:])
    push_east = jnp.concatenate([regridded_exchanges[0][None], blank_levels], axis=0)
    push_north = jnp.concatenate([regridded_exchanges[1][None], blank_levels], axis=0)
    new_east = sea_mask * (zonal_flow + step_ocean * (coriolis_ocean * meridional_flow + visc_ocean * laplace[:levels] + mixing_ocean * vertical(zonal_flow) + push_east))
    new_north = sea_mask * (meridional_flow + step_ocean * (-coriolis_ocean * zonal_flow + visc_ocean * laplace[levels:2 * levels] + mixing_ocean * vertical(meridional_flow) + push_north))
    carried = zonal_flow[0] * east_grad[2 * levels] + meridional_flow[0] * north_grad[2 * levels]
    new_warm = warmth + sea_mask * step_ocean * (heat_gain * regridded_exchanges[2] - carried + diffuse_ocean * laplace[2 * levels])
    return (jnp.stack([new_east, new_north]), new_warm)

def reference(air_winds_heights, exchange_coefficient_air, air_seen_warmness, marine_flow_vectors, marine_warmness, water_indicator, partner_air_tiles, partner_tally_each_tile, partner_overlay_shares):
    joined_quantities = air_winds_heights
    for repeat in range(2):
        joined_quantities = advance(jnp.pad(joined_quantities, ((0, 0), (0, 0), (1, 1), (1, 1))))
    interface_exchanges = uppermost_sheet(joined_quantities, exchange_coefficient_air, air_seen_warmness)
    halves = interface_exchanges.reshape(3, N_TILE, ALAT, N_COMP, ALON).transpose(3, 0, 1, 2, 4).reshape(N_COMP, 3, N_TILE * NAB, BLOCK)
    groups = N_COMP * N_TILE
    sources = partner_air_tiles.reshape(groups, NOB, NOV)
    counts = partner_tally_each_tile.reshape(groups, NOB)
    weights = partner_overlay_shares.reshape(groups, NOB, NOV, BLOCK, BLOCK)
    half_ids = jnp.arange(groups, dtype=jnp.int32) // N_TILE

    def remap_tile(tile_items):
        source_rows, count_rows, weight_rows, half_id = tile_items
        chosen = jnp.take(halves[half_id], source_rows, axis=1)
        return remap_blocks(chosen, count_rows, weight_rows)
    regridded_exchanges = lax.map(remap_tile, (sources, counts, weights, half_ids))
    regridded_exchanges = regridded_exchanges.reshape(N_COMP, N_TILE, 3, OLAT, OLON).transpose(2, 1, 3, 0, 4).reshape(3, MARINE_HEIGHT, MARINE_WIDTH)
    joined_arrays = jnp.concatenate([marine_flow_vectors.reshape(2 * MARINE_DEPTHS, MARINE_HEIGHT, MARINE_WIDTH), marine_warmness[None]], axis=0)
    bordered_argument = jnp.pad(joined_arrays, ((0, 0), (1, 1), (1, 1)))
    advanced_flows, advanced_warmness = marine_drift_advance(bordered_argument, regridded_exchanges, water_indicator.astype(jnp.float32))
    return (joined_quantities, advanced_flows, advanced_warmness)
```

```python
import functools
import jax
import jax.numpy as jnp
from jax import lax
from jax.experimental import pallas as pl
from jax.experimental.pallas import tpu as pltpu
from jax.sharding import PartitionSpec as P

MESH = pl.DeviceIdType.MESH
LANES = 128
HALF = 64

STEP = 0.2
COR = 0.3
VISC = 1.0
MIX = 0.5
GUST = 0.25
HEAT = 1.0
DIFF = 0.5
KEEP = round(1.0 - STEP * (4.0 * VISC + 2.0 * MIX), 12)
assert KEEP == 0.0


def col_roll(v, shift):
    return pltpu.roll(v, shift % v.shape[-1], v.ndim - 1)


def row_roll(v, shift):
    return pltpu.roll(v, shift % v.shape[-2], v.ndim - 2)


def iota(shape, axis):
    return lax.broadcasted_iota(jnp.int32, shape, axis)


def comm_kernel(dims, x, coef, air_warm, flows, warm,
                RN, RS, DNW, DNE, DSW, DSE, CW, CE, ON, OS, CF, CL, RF, RL,
                OF, OL, ssem, rsem):
    F, L, R, W, MR, n_comp, n_tile = dims
    K = F * L
    MF = flows.shape[0] // MR
    c = lax.axis_index("comp")
    t = lax.axis_index("tile")

    def there(dc, dt):
        oks = []
        if dc < 0:
            oks.append(c > 0)
        if dc > 0:
            oks.append(c < n_comp - 1)
        if dt < 0:
            oks.append(t > 0)
        if dt > 0:
            oks.append(t < n_tile - 1)
        ok = oks[0]
        for other in oks[1:]:
            ok = jnp.logical_and(ok, other)
        return ok

    around = [(dc, dt) for dc in (-1, 0, 1) for dt in (-1, 0, 1) if (dc, dt) != (0, 0)]
    barrier = pltpu.get_barrier_semaphore()
    for dc, dt in around:
        @pl.when(there(dc, dt))
        def _(dc=dc, dt=dt):
            pl.semaphore_signal(barrier, inc=1, device_id={"comp": c + dc, "tile": t + dt},
                                device_id_type=MESH)

    for buf, order, edge in ((RF, (0, 1, 2), 0), (RL, (R - 1, R - 2, R - 3), R - 1)):
        for f in range(F):
            for l in range(L):
                for deep in range(2):
                    buf[deep * K + f * L + l:deep * K + f * L + l + 1, :] = x[f, l * R + order[deep]:l * R + order[deep] + 1, :]
            buf[pl.ds(2 * K + f, 1), :] = x[f, pl.ds(order[2], 1), :]
        buf[pl.ds(2 * K + F, 1), :] = coef[pl.ds(edge, 1), :]
        buf[pl.ds(2 * K + F + 1, 1), :] = air_warm[pl.ds(edge, 1), :]
    for buf, row in ((OF, 0), (OL, MR - 1)):
        for k in range(MF):
            buf[k:k + 1, :] = flows[k * MR + row:k * MR + row + 1, :]
        buf[pl.ds(MF, 1), :] = warm[pl.ds(row, 1), :]
    lane = iota((R, LANES), 1)
    mlane = iota((MR, LANES), 1)
    OW = flows.shape[1]
    for buf, at, mat, near, second in ((CF, 0, 0, 0, 1), (CL, W - LANES, OW - LANES, LANES - 1, LANES - 2)):
        acc = jnp.zeros((R, LANES), jnp.float32)
        for k in range(K):
            f, l = divmod(k, L)
            tile = x[f, pl.ds(l * R, R), pl.ds(at, LANES)]
            acc = jnp.where(lane == k, col_roll(tile, k - near), acc)
            acc = jnp.where(lane == HALF + k, col_roll(tile, HALF + k - second), acc)
        buf[pl.ds(0, R), :] = acc
        macc = jnp.zeros((MR, LANES), jnp.float32)
        for k in range(MF + 1):
            if k < MF:
                tile = flows[pl.ds(k * MR, MR), pl.ds(mat, LANES)]
            else:
                tile = warm[:, pl.ds(mat, LANES)]
            macc = jnp.where(mlane == k, col_roll(tile, k - near), macc)
        buf[pl.ds(R, MR), :] = macc

    total = jnp.int32(0)
    for dc, dt in around:
        total = total + there(dc, dt).astype(jnp.int32)
    pl.semaphore_wait(barrier, total)

    first = pl.ds(0, LANES)
    last = pl.ds(W - LANES, LANES)
    plan = [
        (0, -1, RF, RS), (0, 1, RL, RN), (0, -1, OF, OS), (0, 1, OL, ON),
        (-1, 0, CF, CE.at[1]), (1, 0, CL, CW.at[1]),
        (-1, -1, CF, CE.at[2]), (1, -1, CL, CW.at[2]),
        (-1, 1, CF, CE.at[0]), (1, 1, CL, CW.at[0]),
        (-1, -1, RF.at[:, first], DSE), (1, -1, RF.at[:, last], DSW),
        (-1, 1, RL.at[:, first], DNE), (1, 1, RL.at[:, last], DNW),
    ]

    def copy(i):
        dc, dt, src, dst = plan[i]
        return pltpu.make_async_remote_copy(
            src_ref=src, dst_ref=dst, send_sem=ssem.at[i], recv_sem=rsem.at[i],
            device_id={"comp": c + dc, "tile": t + dt}, device_id_type=MESH)

    for i in range(len(plan)):
        @pl.when(there(plan[i][0], plan[i][1]))
        def _(i=i):
            copy(i).start()
    for i in range(len(plan)):
        came = there(-plan[i][0], -plan[i][1])

        @pl.when(jnp.logical_not(came))
        def _(i=i):
            dst = plan[i][3]
            dst[...] = jnp.zeros(dst.shape, jnp.float32)

    for i in range(len(plan)):
        @pl.when(there(-plan[i][0], -plan[i][1]))
        def _(i=i):
            copy(i).wait_recv()

        @pl.when(there(plan[i][0], plan[i][1]))
        def _(i=i):
            copy(i).wait_send()


def update(e, n, h):
    (ec, ep, en, el, er, ev), (nc, np_, nn, nl, nr, nv), (hc, hp, hn, hl, hr, hv) = e, n, h
    new_e = STEP * (COR * nc + ((ep + en) + (el + er)) + 0.5 * (hl - hr + ev))
    new_n = STEP * (-COR * ec + ((np_ + nn) + (nl + nr)) + 0.5 * (hp - hn + nv))
    new_h = STEP * (((hp + hn) + (hl + hr)) + 0.5 * ((el - er) + (np_ - nn) + hv))
    return new_e, new_n, new_h


def main_kernel(dims, part, count, x_hbm, coef, air_warm, flows, warm, water, weights_hbm,
                RN, RS, DNW, DNE, DSW, DSE, CW, CE, ON, OS, CF, CL, RF, RL,
                out_hbm, out_flows, out_warm,
                x, s1, s2, weights, s1n, s1s, s1w, s1e, fx, res, xsem, wsem, osem):
    F, L, R, W, MR, n_comp, n_tile = dims
    K = F * L
    OW = flows.shape[1]
    ML = flows.shape[0] // MR // 2
    NOB, NOV = weights.shape[0], weights.shape[1] // LANES
    CB = W // LANES
    c = lax.axis_index("comp")
    t = lax.axis_index("tile")

    def xcopy(l):
        at = pl.ds(pl.multiple_of(l * R, R), R)
        return pltpu.make_async_copy(x_hbm.at[:, at, :], x.at[:, at, :], xsem.at[l])

    def ocopy(l):
        at = pl.ds(pl.multiple_of(l * R, R), R)
        return pltpu.make_async_copy(s2.at[:, at, :], out_hbm.at[:, at, :], osem)

    @pl.loop(0, L)
    def _(l):
        xcopy(l).start()

    wcopy = pltpu.make_async_copy(weights_hbm, weights, wsem)
    wcopy.start()

    def widen(v, west, east):
        return jnp.concatenate([west, v, east], axis=1)

    def stencil_cols(v, west, east):
        wide = widen(v, west, east)
        return (col_roll(wide, 1)[:, LANES:LANES + v.shape[1]],
                col_roll(wide, -1)[:, LANES:LANES + v.shape[1]])

    def stencil_rows(v, north, south):
        tall = jnp.concatenate([jnp.broadcast_to(north, (8, v.shape[1])), v,
                                jnp.broadcast_to(south, (8, v.shape[1]))], axis=0)
        return row_roll(tall, 1)[8:8 + v.shape[0]], row_roll(tall, -1)[8:8 + v.shape[0]]

    def level(src, l, north, south, west, east):
        parts = []
        for f in range(F):
            k = f * L + l
            v = src[f, pl.ds(pl.multiple_of(l * R, R), R), :]
            up = src[f, pl.ds(pl.multiple_of(jnp.minimum(l + 1, L - 1) * R, R), R), :]
            down = src[f, pl.ds(pl.multiple_of(jnp.maximum(l - 1, 0) * R, R), R), :]
            p, q = stencil_rows(v, north[pl.ds(k, 1), :], south[pl.ds(k, 1), :])
            a, b = stencil_cols(v, pltpu.roll(west, LANES - 1 - k, 1), pltpu.roll(east, lax.rem(LANES - k, LANES), 1))
            parts.append((v, p, q, a, b, up + down))
        return update(*parts)

    cw, ce = CW[1, 0:R, :], CE[1, 0:R, :]

    xcopy(0).wait()

    @pl.loop(0, L)
    def _(l):
        @pl.when(l < L - 1)
        def _():
            xcopy(jnp.minimum(l + 1, L - 1)).wait()

        new = level(x, l, RN, RS, cw, ce)
        for f in range(F):
            s1[f, pl.ds(pl.multiple_of(l * R, R), R), :] = new[f]

    lanes = iota((R, LANES), 1)

    def side(C, own):
        mid = C[1, 0:R, :]
        tall = jnp.concatenate([C[0, 0:R, :], mid, C[2, 0:R, :]], axis=0)
        p, q = row_roll(tall, 1)[R:2 * R], row_roll(tall, -1)[R:2 * R]
        outer = col_roll(mid, -HALF)
        inner = own[0:R, :]
        lev = lanes % L
        up = jnp.where(lev == L - 1, mid, col_roll(mid, -1))
        down = jnp.where(lev == 0, mid, col_roll(mid, 1))
        return mid, p, q, outer, inner, up + down

    def side_step(mid, p, q, a, b, v):
        def moved(f):
            return tuple(col_roll(u, -f * L) for u in (mid, p, q, a, b, v))
        new = update(moved(0), moved(1), moved(2))
        acc = new[0]
        for f in range(1, F):
            acc = jnp.where(lanes >= f * L, col_roll(new[f], f * L), acc)
        return acc

    mid, p, q, a, b, v = side(CW, CF)
    s1w[...] = jnp.where(c > 0, side_step(mid, p, q, a, b, v), 0.0)
    mid, p, q, a, b, v = side(CE, CL)
    s1e[...] = jnp.where(c < n_comp - 1, side_step(mid, p, q, b, a, v), 0.0)

    wide_lanes = iota((1, W + 2 * LANES), 1)
    in_cols = jnp.logical_and(jnp.logical_or(wide_lanes >= LANES, c > 0),
                              jnp.logical_or(wide_lanes < LANES + W, c < n_comp - 1))
    levels = iota((L, W + 2 * LANES), 0)
    tile_lev = iota((L, LANES), 0)
    tile_lane = iota((L, LANES), 1)

    def edge_flux(near, own_row, OWN, valid, DW, D, DE, ring):
        def order(inner, outer):
            return (outer, inner) if near else (inner, outer)

        def both_levels(v):
            return (jnp.where(levels == L - 1, v, row_roll(v, -1))
                    + jnp.where(levels == 0, v, row_roll(v, 1)))

        lo = []
        parts = []
        for f in range(F):
            k = f * L
            center = widen(D[k:k + L, :], DW[k:k + L, :], DE[k:k + L, :])
            outer = widen(D[K + k:K + k + L, :], DW[K + k:K + k + L, :], DE[K + k:K + k + L, :])
            third = widen(D[2 * K + f:2 * K + f + 1, :], DW[2 * K + f:2 * K + f + 1, :],
                          DE[2 * K + f:2 * K + f + 1, :])
            corner_w = jnp.where((tile_lev == 0) & (tile_lane == LANES - 1),
                                 jnp.broadcast_to(CW[1, own_row:own_row + 1, k:k + 1], (L, LANES)), 0.0)
            corner_e = jnp.where((tile_lev == 0) & (tile_lane == 0),
                                 jnp.broadcast_to(CE[1, own_row:own_row + 1, k:k + 1], (L, LANES)), 0.0)
            inner = widen(OWN[k:k + L, :], corner_w, corner_e)
            p, q = order(inner, outer)
            parts.append((center, p, q, col_roll(center, 1), col_roll(center, -1), both_levels(center)))
            far = outer[0:1]
            p, q = order(center[0:1], third)
            lo.append((far, p, q, col_roll(far, 1), col_roll(far, -1), far + outer[1:2]))
        s_near = update(*parts)
        s_far = update(*lo)
        ok = jnp.logical_and(in_cols, valid)
        s_near = [jnp.where(ok, s, 0.0) for s in s_near]
        s_far = [jnp.where(ok, s, 0.0) for s in s_far]
        mids = slice(LANES, LANES + W)
        parts = []
        for f in range(F):
            ring[pl.ds(f * L, L), :] = s_near[f][:, mids]
            v = s_near[f][0:1]
            p, q = order(s1[f, pl.ds(own_row, 1), :], s_far[f][:, mids])
            parts.append((v[:, mids], p, q, col_roll(v, 1)[:, mids], col_roll(v, -1)[:, mids],
                          v[:, mids] + s_near[f][1:2, mids]))
        e, n, h = update(*parts)
        return fluxes(e, n, h, D[2 * K + F:2 * K + F + 1, :], D[2 * K + F + 1:2 * K + F + 2, :])

    def fluxes(e, n, h, co, wa):
        gain = co * jnp.sqrt(e * e + n * n + GUST)
        return gain * e, gain * n, gain * (wa - h)

    def split(flux):
        high = [f.astype(jnp.bfloat16).astype(jnp.float32) for f in flux]
        return high + [f - g for f, g in zip(flux, high)] + [jnp.ones_like(flux[0]), jnp.zeros_like(flux[0])]

    north = split(edge_flux(True, 0, RF, t > 0, DNW, RN, DNE, s1n))
    south = split(edge_flux(False, R - 1, RL, t < n_tile - 1, DSW, RS, DSE, s1s))

    cw, ce = s1w[...], s1e[...]

    @pl.loop(0, L)
    def _(l):
        new = level(s1, l, s1n, s1s, cw, ce)
        for f in range(F):
            s2[f, pl.ds(pl.multiple_of(l * R, R), R), :] = new[f]
        ocopy(l).start()

    own = split(fluxes(s2[0, 0:R, :], s2[1, 0:R, :], s2[2, 0:R, :], coef[...], air_warm[...]))
    for j in range(CB):
        at = slice(j * LANES, (j + 1) * LANES)
        for i in range(8):
            fx[pl.ds(j * 8 + i, 1), :] = north[i][:, at]
            fx[pl.ds((CB + j) * 8 + i, R, stride=CB * 8), :] = own[i][:, at]
            fx[pl.ds(((R + 1) * CB + j) * 8 + i, 1), :] = south[i][:, at]

    wcopy.wait()
    base = (t * R - 1) * CB
    for g in range(NOB):
        tiles = []
        for s in range(NOV):
            row = part[g, s] - base
            tile = fx[pl.ds(pl.multiple_of(row * 8, 8), 8), :]
            tiles.append(jnp.where(s < count[g], tile, 0.0))
        operand = jnp.concatenate(tiles, axis=1).astype(jnp.bfloat16)
        res[pl.ds(g * 8, 8), :] = jnp.dot(operand, weights[g], preferred_element_type=jnp.float32)

    cols = OW // LANES

    def gathered(i):
        return jnp.concatenate([res[pl.ds(q * 8 + i, MR, stride=cols * 8), :] for q in range(cols)], axis=1)

    below = gathered(2 * F)
    push = [(gathered(f) + gathered(F + f)) / below for f in range(F)]

    mask = water[...].astype(jnp.float32)
    ow, oe = CW[1, R:R + MR, :], CE[1, R:R + MR, :]

    def around(k, v):
        p, q = stencil_rows(v, ON[k:k + 1, :], OS[k:k + 1, :])
        a, b = stencil_cols(v, col_roll(ow, LANES - 1 - k), col_roll(oe, -k))
        return p, q, a, b

    for l in range(ML):
        E = flows[l * MR:(l + 1) * MR, :]
        N = flows[(ML + l) * MR:(ML + l + 1) * MR, :]
        for which, own_v, turned in ((0, E, COR * N), (1, N, -COR * E)):
            k = which * ML + l
            p, q, a, b = around(k, own_v)
            hi = which * ML + min(l + 1, ML - 1)
            lo = which * ML + max(l - 1, 0)
            both = flows[hi * MR:(hi + 1) * MR, :] + flows[lo * MR:(lo + 1) * MR, :]
            total = turned + ((p + q) + (a + b)) + 0.5 * both
            if l == 0:
                total = total + push[which]
            out_flows[k * MR:(k + 1) * MR, :] = mask * (STEP * total)
    T = warm[...]
    p, q, a, b = around(2 * ML, T)
    carried = flows[0:MR, :] * (0.5 * (b - a)) + flows[ML * MR:(ML + 1) * MR, :] * (0.5 * (q - p))
    lap = (p + q) + (a + b) - 4.0 * T
    out_warm[...] = T + mask * STEP * (HEAT * push[2] - carried + DIFF * lap)

    pltpu.make_async_copy(s2, out_hbm, osem).wait()


def shards(n_comp, n_tile, air, coef, air_warm, flows, warm, water, part, count, shares):
    F, L, R, W = air.shape
    MR, OW = warm.shape
    MF = flows.shape[0] * flows.shape[1]
    NOB, NOV = part.shape
    K = F * L
    dims = (F, L, R, W, MR, n_comp, n_tile)
    x = air.reshape(F, L * R, W)
    flows2 = flows.reshape(MF * MR, OW)
    rows = 2 * K + 8
    orows = -(-(MF + 1) // 8) * 8
    f32 = jnp.float32
    sds = jax.ShapeDtypeStruct
    vm = pl.BlockSpec(memory_space=pltpu.VMEM)
    sm = pl.BlockSpec(memory_space=pltpu.SMEM)
    hb = pl.BlockSpec(memory_space=pl.ANY)
    halos = ([(rows, W)] * 2 + [(rows, LANES)] * 4 + [(3, R + MR, LANES)] * 2 + [(orows, OW)] * 2
             + [(R + MR, LANES)] * 2 + [(rows, W)] * 2)
    got = pl.pallas_call(
        functools.partial(comm_kernel, dims),
        out_shape=[sds(s, f32) for s in halos],
        in_specs=[vm] * 5,
        out_specs=[vm] * len(halos),
        scratch_shapes=[pltpu.VMEM((orows, OW), f32)] * 2
        + [pltpu.SemaphoreType.DMA((14,))] * 2,
        compiler_params=pltpu.CompilerParams(collective_id=0, has_side_effects=True),
        name="halo",
    )(x, coef, air_warm, flows2, warm)
    nxt, new_flows, new_warm = pl.pallas_call(
        functools.partial(main_kernel, dims),
        out_shape=[sds(x.shape, f32), sds(flows2.shape, f32), sds(warm.shape, f32)],
        in_specs=[sm, sm, hb] + [vm] * 5 + [hb] + [vm] * len(halos),
        out_specs=[hb, vm, vm],
        scratch_shapes=[pltpu.VMEM(x.shape, f32)] * 3
        + [pltpu.VMEM((NOB, NOV * LANES, LANES), jnp.bfloat16)]
        + [pltpu.VMEM((K, W), f32)] * 2
        + [pltpu.VMEM((R, LANES), f32)] * 2
        + [pltpu.VMEM(((R + 2) * (W // LANES) * 8, LANES), f32), pltpu.VMEM((NOB * 8, LANES), f32)]
        + [pltpu.SemaphoreType.DMA((L,)), pltpu.SemaphoreType.DMA, pltpu.SemaphoreType.DMA],
        compiler_params=pltpu.CompilerParams(vmem_limit_bytes=48 << 20),
        name="window",
    )(part, count, x, coef, air_warm, flows2, warm, water,
      shares.reshape(NOB, NOV * LANES, LANES), *got)
    return nxt.reshape(air.shape), new_flows.reshape(flows.shape), new_warm


def solution(mesh):
    placed = (
        P(None, None, "tile", "comp"),
        P("tile", "comp"),
        P("tile", "comp"),
        P(None, None, "tile", "comp"),
        P("tile", "comp"),
        P("tile", "comp"),
        P(("comp", "tile"), None),
        P(("comp", "tile")),
        P(("comp", "tile"), None, None, None),
    )
    return jax.shard_map(
        functools.partial(shards, mesh.shape["comp"], mesh.shape["tile"]),
        mesh=mesh,
        in_specs=placed,
        out_specs=(P(None, None, "tile", "comp"), P(None, None, "tile", "comp"), P("tile", "comp")),
        check_vma=False,
    )
```

```python
import functools
import jax
import jax.numpy as jnp
from jax import lax
from jax.experimental import pallas as pl
from jax.experimental.pallas import tpu as pltpu
from jax.sharding import PartitionSpec as P

MESH = pl.DeviceIdType.MESH
LANES = 128
HALF = 64

STEP = 0.2
COR = 0.3
VISC = 1.0
MIX = 0.5
GUST = 0.25
HEAT = 1.0
DIFF = 0.5
KEEP = round(1.0 - STEP * (4.0 * VISC + 2.0 * MIX), 12)
assert KEEP == 0.0


def col_roll(v, shift):
    return pltpu.roll(v, shift % v.shape[-1], v.ndim - 1)


def row_roll(v, shift):
    return pltpu.roll(v, shift % v.shape[-2], v.ndim - 2)


def iota(shape, axis):
    return lax.broadcasted_iota(jnp.int32, shape, axis)


def update(e, n, h):
    (ec, ep, en, el, er, ev), (nc, np_, nn, nl, nr, nv), (hc, hp, hn, hl, hr, hv) = e, n, h
    new_e = STEP * (COR * nc + ((ep + en) + (el + er)) + 0.5 * (hl - hr + ev))
    new_n = STEP * (-COR * ec + ((np_ + nn) + (nl + nr)) + 0.5 * (hp - hn + nv))
    new_h = STEP * (((hp + hn) + (hl + hr)) + 0.5 * ((el - er) + (np_ - nn) + hv))
    return new_e, new_n, new_h


def window_kernel(dims, part_hbm, count_hbm, x_hbm, coef_hbm, air_warm_hbm, flows_hbm, warm_hbm, water_hbm, weights_hbm,
                  out_hbm, out_flows_hbm, out_warm_hbm,
                  part, count, x, coef, air_warm, flows, warm, water, weights, out_flows, out_warm,
                  RN, RS, DNW, DNE, DSW, DSE, CW, CE, ON, OS, CF, CL, RF, RL, OF, OL,
                  s1, s2, s1n, s1s, fixn, fixs, s1w, s1e, fixw, fixe, fx, res,
                  xsem, insem, osem, ssem, rsem):
    F, L, R, W, MR, n_comp, n_tile = dims
    H = L // 2
    MF = flows.shape[0] // MR
    ML = MF // 2
    OW = flows.shape[1]
    NOB, NOV = weights.shape[0], weights.shape[1] // LANES
    CB = W // LANES
    FH = F * H
    EXTRA = 2 * FH
    EARLY = EXTRA + 8
    c = lax.axis_index("comp")
    t = lax.axis_index("tile")

    def there(dc, dt):
        oks = []
        if dc < 0:
            oks.append(c > 0)
        if dc > 0:
            oks.append(c < n_comp - 1)
        if dt < 0:
            oks.append(t > 0)
        if dt > 0:
            oks.append(t < n_tile - 1)
        ok = oks[0]
        for other in oks[1:]:
            ok = jnp.logical_and(ok, other)
        return ok

    around = [(dc, dt) for dc in (-1, 0, 1) for dt in (-1, 0, 1) if (dc, dt) != (0, 0)]
    barrier = pltpu.get_barrier_semaphore()
    for dc, dt in around:
        @pl.when(there(dc, dt))
        def _(dc=dc, dt=dt):
            pl.semaphore_signal(barrier, inc=1, device_id={"comp": c + dc, "tile": t + dt},
                                device_id_type=MESH)

    def rows_of(l):
        return pl.ds(pl.multiple_of(l * R, R), R)

    def xcopy(l):
        at = rows_of(l)
        return pltpu.make_async_copy(x_hbm.at[:, at, :], x.at[:, at, :], xsem.at[l])

    def ocopy(l):
        at = rows_of(l)
        return pltpu.make_async_copy(s2.at[:, at, :], out_hbm.at[:, at, :], osem.at[0])

    for l in range(L):
        xcopy(l).start()
    incopies = [pltpu.make_async_copy(src, dst, insem.at[i]) for i, (src, dst) in enumerate((
        (coef_hbm, coef), (air_warm_hbm, air_warm), (flows_hbm, flows), (warm_hbm, warm),
        (water_hbm, water), (part_hbm, part), (count_hbm, count), (weights_hbm, weights)))]
    for copy in incopies:
        copy.start()

    def slot(f, l, deep):
        return deep * FH + f * H + l if l < H else EARLY + deep * FH + f * H + l - H

    edges = ((RF, (0, 1, 2), 0), (RL, (R - 1, R - 2, R - 3), R - 1))

    def pack_rows(levels):
        for buf, order, _ in edges:
            for f in range(F):
                for l in levels:
                    for deep in range(2):
                        at = slot(f, l, deep)
                        buf[at:at + 1, :] = x[f, l * R + order[deep]:l * R + order[deep] + 1, :]

    first = pl.ds(0, LANES)
    last = pl.ds(W - LANES, LANES)
    early = pl.ds(0, EARLY)
    late = pl.ds(EARLY, 2 * FH)
    plan = [
        (0, -1, RF.at[early], RS.at[early]), (0, 1, RL.at[early], RN.at[early]),
        (-1, 0, CF, CE.at[1]), (1, 0, CL, CW.at[1]),
        (-1, -1, CF, CE.at[2]), (1, -1, CL, CW.at[2]),
        (-1, 1, CF, CE.at[0]), (1, 1, CL, CW.at[0]),
        (-1, -1, RF.at[:, first], DSE), (1, -1, RF.at[:, last], DSW),
        (-1, 1, RL.at[:, first], DNE), (1, 1, RL.at[:, last], DNW),
        (0, -1, OF, OS), (0, 1, OL, ON),
        (0, -1, RF.at[late], RS.at[late]), (0, 1, RL.at[late], RN.at[late]),
    ]
    LATE = (14, 15)

    def copy(i):
        dc, dt, src, dst = plan[i]
        return pltpu.make_async_remote_copy(
            src_ref=src, dst_ref=dst, send_sem=ssem.at[i], recv_sem=rsem.at[i],
            device_id={"comp": c + dc, "tile": t + dt}, device_id_type=MESH)

    def send(i):
        @pl.when(there(plan[i][0], plan[i][1]))
        def _():
            copy(i).start()

    def receive(i):
        @pl.when(there(-plan[i][0], -plan[i][1]))
        def _():
            copy(i).wait_recv()

    for l in range(H):
        xcopy(l).wait()
    incopies[0].wait()
    incopies[1].wait()
    pack_rows(range(H))
    for buf, order, edge in edges:
        for f in range(F):
            buf[EXTRA + f:EXTRA + f + 1, :] = x[f, order[2]:order[2] + 1, :]
        buf[EXTRA + F:EXTRA + F + 1, :] = coef[edge:edge + 1, :]
        buf[EXTRA + F + 1:EXTRA + F + 2, :] = air_warm[edge:edge + 1, :]

    total = jnp.int32(0)
    for dc, dt in around:
        total = total + there(dc, dt).astype(jnp.int32)
    pl.semaphore_wait(barrier, total)
    send(0)
    send(1)

    for l in range(H, L):
        xcopy(l).wait()
    incopies[2].wait()
    incopies[3].wait()
    lanes = iota((R, LANES), 1)
    mlane = iota((MR, LANES), 1)
    for buf, at, mat, near, second in ((CF, 0, 0, 0, 1), (CL, W - LANES, OW - LANES, LANES - 1, LANES - 2)):
        acc = jnp.zeros((R, LANES), jnp.float32)
        for k in range(F * L):
            f, l = divmod(k, L)
            tile = x[f, pl.ds(l * R, R), pl.ds(at, LANES)]
            acc = jnp.where(lanes == k, col_roll(tile, k - near), acc)
            acc = jnp.where(lanes == HALF + k, col_roll(tile, HALF + k - second), acc)
        buf[pl.ds(0, R), :] = acc
        macc = jnp.zeros((MR, LANES), jnp.float32)
        for k in range(MF + 1):
            tile = flows[pl.ds(k * MR, MR), pl.ds(mat, LANES)] if k < MF else warm[:, pl.ds(mat, LANES)]
            macc = jnp.where(mlane == k, col_roll(tile, k - near), macc)
        buf[pl.ds(R, MR), :] = macc
    for i in range(2, 8):
        send(i)
    pack_rows(range(H, L))
    for buf, row in ((OF, 0), (OL, MR - 1)):
        for k in range(MF):
            buf[k:k + 1, :] = flows[k * MR + row:k * MR + row + 1, :]
        buf[MF:MF + 1, :] = warm[row:row + 1, :]
    for i in range(8, len(plan)):
        send(i)
    for i in range(len(plan)):
        @pl.when(jnp.logical_not(there(-plan[i][0], -plan[i][1])))
        def _(i=i):
            dst = plan[i][3]
            dst[...] = jnp.zeros(dst.shape, jnp.float32)

    rowid = iota((R, W), 0)
    colid = iota((R, W), 1)

    def beside_rows(v, north, south):
        ids = rowid[0:v.shape[0], 0:v.shape[1]]
        return (jnp.where(ids == 0, north, row_roll(v, 1)),
                jnp.where(ids == v.shape[0] - 1, south, row_roll(v, -1)))

    def widen(v, west, east):
        return jnp.concatenate([west, v, east], axis=1)

    def beside_cols(v, west, east):
        wide = widen(v, west, east)
        return (col_roll(wide, 1)[:, LANES:LANES + v.shape[1]],
                col_roll(wide, -1)[:, LANES:LANES + v.shape[1]])

    def self_and_levels(src, f, l):
        v = src[f, rows_of(l), :]
        return v, src[f, rows_of(jnp.minimum(l + 1, L - 1)), :] + src[f, rows_of(jnp.maximum(l - 1, 0)), :]

    @pl.loop(0, L)
    def _(l):
        parts = []
        for f in range(F):
            v, both = self_and_levels(x, f, l)
            p, q = beside_rows(v, 0.0, 0.0)
            a = jnp.where(colid == 0, 0.0, col_roll(v, 1))
            b = jnp.where(colid == W - 1, 0.0, col_roll(v, -1))
            parts.append((v, p, q, a, b, both))
        new = update(*parts)
        for f in range(F):
            s1[f, rows_of(l), :] = new[f]

    def halo(D, f, deep, half):
        at = slot(f, half * H, deep)
        return D[at:at + H, :]

    def fix_rows(half):
        for D, fix, sign in ((RN, fixn, 0.5), (RS, fixs, -0.5)):
            e, n, h = (halo(D, f, 0, half) for f in range(F))
            for f, v in enumerate((e, n + sign * h, h + sign * n)):
                fix[f * L + half * H:f * L + half * H + H, :] = STEP * v

    def fix_cols():
        for C, fix, sign in ((CW, fixw, 0.5), (CE, fixe, -0.5)):
            mid = C[1, 0:R, :]
            v = jnp.where(lanes < L, mid + sign * col_roll(mid, -2 * L), mid)
            v = jnp.where(lanes >= 2 * L, mid + sign * col_roll(mid, 2 * L), v)
            fix[...] = STEP * v

    row8 = iota((8, W), 0)

    def add_fixes(lo, hi):
        west, east = fixw[...], fixe[...]

        @pl.loop(lo, hi)
        def _(l):
            for f in range(F):
                k = f * L + l
                top = pl.ds(pl.multiple_of(l * R, R), 8)
                low = pl.ds(pl.multiple_of(l * R + R - 8, 8), 8)
                s1[f, top, :] = s1[f, top, :] + jnp.where(row8 == 0, fixn[pl.ds(k, 1), :], 0.0)
                s1[f, low, :] = s1[f, low, :] + jnp.where(row8 == 7, fixs[pl.ds(k, 1), :], 0.0)
                at = rows_of(l)
                s1[f, at, first] = s1[f, at, first] + jnp.where(
                    lanes == 0, pltpu.roll(west, lax.rem(LANES - k, LANES), 1), 0.0)
                s1[f, at, last] = s1[f, at, last] + jnp.where(
                    lanes == LANES - 1, pltpu.roll(east, LANES - 1 - k, 1), 0.0)

    def side(C, own):
        mid = C[1, 0:R, :]
        tall = jnp.concatenate([C[0, 0:R, :], mid, C[2, 0:R, :]], axis=0)
        p, q = row_roll(tall, 1)[R:2 * R], row_roll(tall, -1)[R:2 * R]
        outer = col_roll(mid, -HALF)
        inner = own[0:R, :]
        lev = lanes % L
        up = jnp.where(lev == L - 1, mid, col_roll(mid, -1))
        down = jnp.where(lev == 0, mid, col_roll(mid, 1))
        return mid, p, q, outer, inner, up + down

    def side_step(mid, p, q, a, b, v):
        def moved(f):
            return tuple(col_roll(u, -f * L) for u in (mid, p, q, a, b, v))
        new = update(moved(0), moved(1), moved(2))
        acc = new[0]
        for f in range(1, F):
            acc = jnp.where(lanes >= f * L, col_roll(new[f], f * L), acc)
        return acc

    wide_lanes = iota((1, W + 2 * LANES), 1)
    in_cols = jnp.logical_and(jnp.logical_or(wide_lanes >= LANES, c > 0),
                              jnp.logical_or(wide_lanes < LANES + W, c < n_comp - 1))
    mids = slice(LANES, LANES + W)
    north_of = (True, 0, RF, t > 0, DNW, RN, DNE, s1n)
    south_of = (False, R - 1, RL, t < n_tile - 1, DSW, RS, DSE, s1s)

    def ring_rows(where_, halves):
        near, own_row, OWN, valid, DW, D, DE, ring = where_
        n = halves * H
        lev = iota((n, W + 2 * LANES), 0)
        tlev = iota((n, LANES), 0)
        tlane = iota((n, LANES), 1)

        def stacked(buf, f, deep):
            return jnp.concatenate([halo(buf, f, deep, i) for i in range(halves)], axis=0)

        parts, outers = [], []
        for f in range(F):
            k = f * L
            center = widen(stacked(D, f, 0), stacked(DW, f, 0), stacked(DE, f, 0))
            outer = widen(stacked(D, f, 1), stacked(DW, f, 1), stacked(DE, f, 1))
            west = jnp.where((tlev == 0) & (tlane == LANES - 1),
                             jnp.broadcast_to(CW[1, own_row:own_row + 1, k:k + 1], (n, LANES)), 0.0)
            east = jnp.where((tlev == 0) & (tlane == 0),
                             jnp.broadcast_to(CE[1, own_row:own_row + 1, k:k + 1], (n, LANES)), 0.0)
            inner = widen(stacked(OWN, f, 0), west, east)
            p, q = (outer, inner) if near else (inner, outer)
            both = (jnp.where(lev == n - 1, center, row_roll(center, -1))
                    + jnp.where(lev == 0, center, row_roll(center, 1)))
            parts.append((center, p, q, col_roll(center, 1), col_roll(center, -1), both))
            outers.append(outer)
        ok = jnp.logical_and(in_cols, valid)
        new = [jnp.where(ok, s, 0.0) for s in update(*parts)]
        for f in range(F):
            ring[f * L:f * L + n, :] = new[f][:, mids]
        return new, [p[0] for p in parts], outers

    def fluxes(e, n, h, co, wa):
        gain = co * jnp.sqrt(e * e + n * n + GUST)
        return gain * e, gain * n, gain * (wa - h)

    def edge_flux(where_):
        near, own_row, OWN, valid, DW, D, DE, ring = where_
        s_near, centers, outers = ring_rows(where_, 1)
        parts = []
        for f in range(F):
            at = slice(EXTRA + f, EXTRA + f + 1)
            third = widen(D[at, :], DW[at, :], DE[at, :])
            far = outers[f][0:1]
            p, q = (third, centers[f][0:1]) if near else (centers[f][0:1], third)
            parts.append((far, p, q, col_roll(far, 1), col_roll(far, -1), far + outers[f][1:2]))
        s_far = update(*parts)
        parts = []
        for f in range(F):
            v = s_near[f][0:1]
            inner = s1[f, pl.ds(own_row, 1), :]
            p, q = (s_far[f][:, mids], inner) if near else (inner, s_far[f][:, mids])
            parts.append((v[:, mids], p, q, col_roll(v, 1)[:, mids], col_roll(v, -1)[:, mids],
                          v[:, mids] + s_near[f][1:2, mids]))
        e, n, h = update(*parts)
        return fluxes(e, n, h, D[EXTRA + F:EXTRA + F + 1, :], D[EXTRA + F + 1:EXTRA + F + 2, :])

    def split(flux):
        high = [f.astype(jnp.bfloat16).astype(jnp.float32) for f in flux]
        return high + [f - g for f, g in zip(flux, high)] + [jnp.ones_like(flux[0]), jnp.zeros_like(flux[0])]

    def second(l):
        west, east = s1w[...], s1e[...]
        parts = []
        for f in range(F):
            k = f * L + l
            v, both = self_and_levels(s1, f, l)
            p, q = beside_rows(v, s1n[pl.ds(k, 1), :], s1s[pl.ds(k, 1), :])
            a, b = beside_cols(v, pltpu.roll(west, LANES - 1 - k, 1), pltpu.roll(east, lax.rem(LANES - k, LANES), 1))
            parts.append((v, p, q, a, b, both))
        new = update(*parts)
        for f in range(F):
            s2[f, rows_of(l), :] = new[f]
        ocopy(l).start()

    for i in range(len(plan)):
        if i not in LATE:
            receive(i)
    mid, p, q, a, b, v = side(CW, CF)
    s1w[...] = jnp.where(c > 0, side_step(mid, p, q, a, b, v), 0.0)
    mid, p, q, a, b, v = side(CE, CL)
    s1e[...] = jnp.where(c < n_comp - 1, side_step(mid, p, q, b, a, v), 0.0)
    fix_cols()
    fix_rows(0)
    add_fixes(0, H)
    north = split(edge_flux(north_of))
    south = split(edge_flux(south_of))

    @pl.loop(0, H - 1)
    def _(l):
        second(l)

    own = split(fluxes(s2[0, 0:R, :], s2[1, 0:R, :], s2[2, 0:R, :], coef[...], air_warm[...]))
    for j in range(CB):
        at = slice(j * LANES, (j + 1) * LANES)
        for i in range(8):
            fx[j, i:i + 1, :] = north[i][:, at]
            fx[pl.ds(CB + j, R, stride=CB), i, :] = own[i][:, at]
            fx[(R + 1) * CB + j, i:i + 1, :] = south[i][:, at]

    for copy_in in incopies[4:]:
        copy_in.wait()
    base = (t * R - 1) * CB
    for g in range(NOB):
        tiles = []
        for s in range(NOV):
            live = jnp.clip(count[0, g] - s, 0, 1).astype(jnp.float32)
            tiles.append(fx[jnp.clip(part[s, g] - base, 0, fx.shape[0] - 1)] * live)
        operand = jnp.concatenate(tiles, axis=1).astype(jnp.bfloat16)
        res[pl.ds(g * 8, 8), :] = jnp.dot(operand, weights[g], preferred_element_type=jnp.float32)

    cols = OW // LANES

    def gathered(i):
        return jnp.concatenate([res[pl.ds(q * 8 + i, MR, stride=cols * 8), :] for q in range(cols)], axis=1)

    below = gathered(2 * F)
    push = [(gathered(f) + gathered(F + f)) / below for f in range(F)]

    mask = water[...].astype(jnp.float32)
    ow, oe = CW[1, R:R + MR, :], CE[1, R:R + MR, :]

    def neighbours(k, v):
        p, q = beside_rows(v, ON[k:k + 1, :], OS[k:k + 1, :])
        a, b = beside_cols(v, col_roll(ow, LANES - 1 - k), col_roll(oe, -k))
        return p, q, a, b

    for l in range(ML):
        E = flows[l * MR:(l + 1) * MR, :]
        N = flows[(ML + l) * MR:(ML + l + 1) * MR, :]
        for which, own_v, turned in ((0, E, COR * N), (1, N, -COR * E)):
            k = which * ML + l
            p, q, a, b = neighbours(k, own_v)
            hi = which * ML + min(l + 1, ML - 1)
            lo = which * ML + max(l - 1, 0)
            both = flows[hi * MR:(hi + 1) * MR, :] + flows[lo * MR:(lo + 1) * MR, :]
            total = turned + ((p + q) + (a + b)) + 0.5 * both
            if l == 0:
                total = total + push[which]
            out_flows[k * MR:(k + 1) * MR, :] = mask * (STEP * total)
    T = warm[...]
    p, q, a, b = neighbours(2 * ML, T)
    carried = flows[0:MR, :] * (0.5 * (b - a)) + flows[ML * MR:(ML + 1) * MR, :] * (0.5 * (q - p))
    lap = (p + q) + (a + b) - 4.0 * T
    out_warm[...] = T + mask * STEP * (HEAT * push[2] - carried + DIFF * lap)
    outs = [pltpu.make_async_copy(out_flows, out_flows_hbm, osem.at[1]),
            pltpu.make_async_copy(out_warm, out_warm_hbm, osem.at[2])]
    for copy_out in outs:
        copy_out.start()

    for i in LATE:
        receive(i)
    fix_rows(1)
    add_fixes(H, L)
    ring_rows(north_of, 2)
    ring_rows(south_of, 2)

    @pl.loop(H - 1, L)
    def _(l):
        second(l)

    for i in range(len(plan)):
        @pl.when(there(plan[i][0], plan[i][1]))
        def _(i=i):
            copy(i).wait_send()
    for copy_out in outs:
        copy_out.wait()
    pltpu.make_async_copy(s2, out_hbm, osem.at[0]).wait()


def shards(n_comp, n_tile, air, coef, air_warm, flows, warm, water, part, count, shares):
    F, L, R, W = air.shape
    MR, OW = warm.shape
    MF = flows.shape[0] * flows.shape[1]
    NOB, NOV = part.shape
    K = F * L
    dims = (F, L, R, W, MR, n_comp, n_tile)
    x = air.reshape(F, L * R, W)
    flows2 = flows.reshape(MF * MR, OW)
    rows = 2 * K + 8
    orows = -(-(MF + 1) // 8) * 8
    f32 = jnp.float32
    sds = jax.ShapeDtypeStruct
    hb = pl.BlockSpec(memory_space=pl.ANY)
    wshape = (NOB, NOV * LANES, LANES)
    halos = ([(rows, W)] * 2 + [(rows, LANES)] * 4 + [(3, R + MR, LANES)] * 2 + [(orows, OW)] * 2
             + [(R + MR, LANES)] * 2 + [(rows, W)] * 2 + [(orows, OW)] * 2)
    work = ([x.shape] * 2 + [(K, W)] * 4 + [(R, LANES)] * 4
            + [((R + 2) * (W // LANES), 8, LANES), (NOB * 8, LANES)])
    vf = [pltpu.VMEM(s, f32) for s in halos + work]
    nxt, new_flows, new_warm = pl.pallas_call(
        functools.partial(window_kernel, dims),
        out_shape=[sds(x.shape, f32), sds(flows2.shape, f32), sds(warm.shape, f32)],
        in_specs=[hb] * 9,
        out_specs=[hb] * 3,
        scratch_shapes=[
            pltpu.SMEM((NOV, NOB), jnp.int32), pltpu.SMEM((1, NOB), jnp.int32),
            pltpu.VMEM(x.shape, f32), pltpu.VMEM(coef.shape, f32), pltpu.VMEM(coef.shape, f32),
            pltpu.VMEM(flows2.shape, f32), pltpu.VMEM(warm.shape, f32), pltpu.VMEM(warm.shape, jnp.int32),
            pltpu.VMEM(wshape, jnp.bfloat16), pltpu.VMEM(flows2.shape, f32), pltpu.VMEM(warm.shape, f32)]
        + vf
        + [pltpu.SemaphoreType.DMA((L,)), pltpu.SemaphoreType.DMA((8,)), pltpu.SemaphoreType.DMA((3,)),
           pltpu.SemaphoreType.DMA((16,)), pltpu.SemaphoreType.DMA((16,))],
        compiler_params=pltpu.CompilerParams(collective_id=0, has_side_effects=True, vmem_limit_bytes=60 << 20),
        name="window",
    )(part.T, count.reshape(1, NOB), x, coef, air_warm, flows2, warm, water, shares.reshape(wshape))
    return nxt.reshape(air.shape), new_flows.reshape(flows.shape), new_warm


def solution(mesh):
    placed = (
        P(None, None, "tile", "comp"),
        P("tile", "comp"),
        P("tile", "comp"),
        P(None, None, "tile", "comp"),
        P("tile", "comp"),
        P("tile", "comp"),
        P(("comp", "tile"), None),
        P(("comp", "tile")),
        P(("comp", "tile"), None, None, None),
    )
    return jax.shard_map(
        functools.partial(shards, mesh.shape["comp"], mesh.shape["tile"]),
        mesh=mesh,
        in_specs=placed,
        out_specs=(P(None, None, "tile", "comp"), P(None, None, "tile", "comp"), P("tile", "comp")),
        check_vma=False,
    )
```

```python
import functools
import jax
import jax.numpy as jnp
from jax import lax
from jax.experimental import pallas as pl
from jax.experimental.pallas import tpu as pltpu
from jax.sharding import PartitionSpec as P

MESH = pl.DeviceIdType.MESH
LANES = 128
HALF = 64

STEP = 0.2
COR = 0.3
VISC = 1.0
MIX = 0.5
GUST = 0.25
HEAT = 1.0
DIFF = 0.5
KEEP = round(1.0 - STEP * (4.0 * VISC + 2.0 * MIX), 12)
assert KEEP == 0.0


def col_roll(v, shift):
    return pltpu.roll(v, shift % v.shape[-1], v.ndim - 1)


def row_roll(v, shift):
    return pltpu.roll(v, shift % v.shape[-2], v.ndim - 2)


def iota(shape, axis):
    return lax.broadcasted_iota(jnp.int32, shape, axis)


def update(e, n, h):
    (ec, ep, en, el, er, ev), (nc, np_, nn, nl, nr, nv), (hc, hp, hn, hl, hr, hv) = e, n, h
    new_e = STEP * (COR * nc + ((ep + en) + (el + er)) + 0.5 * (hl - hr + ev))
    new_n = STEP * (-COR * ec + ((np_ + nn) + (nl + nr)) + 0.5 * (hp - hn + nv))
    new_h = STEP * (((hp + hn) + (hl + hr)) + 0.5 * ((el - er) + (np_ - nn) + hv))
    return new_e, new_n, new_h


def window_kernel(dims, part_hbm, count_hbm, x_hbm, coef_hbm, air_warm_hbm, flows_hbm, warm_hbm, water_hbm, weights_hbm,
                  out_hbm, out_flows_hbm, out_warm_hbm,
                  part, count, x, coef, air_warm, flows, warm, water, weights, out_flows, out_warm,
                  RN, RS, DNW, DNE, DSW, DSE, CW, CE, ON, OS, CF, CL, RF, RL, OF, OL,
                  s1, s2, s1n, s1s, fixn, fixs, s1w, s1e, fixw, fixe, fx, res,
                  xsem, insem, osem, ssem, rsem):
    F, L, R, W, MR, n_comp, n_tile = dims
    H = L // 2
    MF = flows.shape[0] // MR
    ML = MF // 2
    OW = flows.shape[1]
    NOB, NOV = weights.shape[0], weights.shape[1] // LANES
    CB = W // LANES
    FH = F * H
    EXTRA = 2 * FH
    EARLY = EXTRA + 8
    c = lax.axis_index("comp")
    t = lax.axis_index("tile")

    def there(dc, dt):
        oks = []
        if dc < 0:
            oks.append(c > 0)
        if dc > 0:
            oks.append(c < n_comp - 1)
        if dt < 0:
            oks.append(t > 0)
        if dt > 0:
            oks.append(t < n_tile - 1)
        ok = oks[0]
        for other in oks[1:]:
            ok = jnp.logical_and(ok, other)
        return ok

    around = [(dc, dt) for dc in (-1, 0, 1) for dt in (-1, 0, 1) if (dc, dt) != (0, 0)]
    barrier = pltpu.get_barrier_semaphore()
    for dc, dt in around:
        @pl.when(there(dc, dt))
        def _(dc=dc, dt=dt):
            pl.semaphore_signal(barrier, inc=1, device_id={"comp": c + dc, "tile": t + dt},
                                device_id_type=MESH)

    def rows_of(l):
        return pl.ds(pl.multiple_of(l * R, R), R)

    def xcopy(l):
        at = rows_of(l)
        return pltpu.make_async_copy(x_hbm.at[:, at, :], x.at[:, at, :], xsem.at[l])

    def ocopy(l):
        at = rows_of(l)
        return pltpu.make_async_copy(s2.at[:, at, :], out_hbm.at[:, at, :], osem.at[0])

    for l in range(L):
        xcopy(l).start()
    incopies = [pltpu.make_async_copy(src, dst, insem.at[i]) for i, (src, dst) in enumerate((
        (coef_hbm, coef), (air_warm_hbm, air_warm), (flows_hbm, flows), (warm_hbm, warm),
        (water_hbm, water), (part_hbm, part), (count_hbm, count), (weights_hbm, weights)))]
    for copy in incopies:
        copy.start()

    def slot(f, l, deep):
        return deep * FH + f * H + l if l < H else EARLY + deep * FH + f * H + l - H

    edges = ((RF, (0, 1, 2), 0), (RL, (R - 1, R - 2, R - 3), R - 1))

    def pack_rows(levels):
        for buf, order, _ in edges:
            for f in range(F):
                for l in levels:
                    for deep in range(2):
                        at = slot(f, l, deep)
                        buf[at:at + 1, :] = x[f, l * R + order[deep]:l * R + order[deep] + 1, :]

    first = pl.ds(0, LANES)
    last = pl.ds(W - LANES, LANES)
    early = pl.ds(0, EARLY)
    late = pl.ds(EARLY, 2 * FH)
    plan = [
        (0, -1, RF.at[early], RS.at[early]), (0, 1, RL.at[early], RN.at[early]),
        (-1, 0, CF, CE.at[1]), (1, 0, CL, CW.at[1]),
        (-1, -1, CF, CE.at[2]), (1, -1, CL, CW.at[2]),
        (-1, 1, CF, CE.at[0]), (1, 1, CL, CW.at[0]),
        (-1, -1, RF.at[:, first], DSE), (1, -1, RF.at[:, last], DSW),
        (-1, 1, RL.at[:, first], DNE), (1, 1, RL.at[:, last], DNW),
        (0, -1, OF, OS), (0, 1, OL, ON),
        (0, -1, RF.at[late], RS.at[late]), (0, 1, RL.at[late], RN.at[late]),
    ]
    LATE = (14, 15)

    def copy(i):
        dc, dt, src, dst = plan[i]
        return pltpu.make_async_remote_copy(
            src_ref=src, dst_ref=dst, send_sem=ssem.at[i], recv_sem=rsem.at[i],
            device_id={"comp": c + dc, "tile": t + dt}, device_id_type=MESH)

    def send(i):
        @pl.when(there(plan[i][0], plan[i][1]))
        def _():
            copy(i).start()

    def receive(i):
        @pl.when(there(-plan[i][0], -plan[i][1]))
        def _():
            copy(i).wait_recv()

    for l in range(H):
        xcopy(l).wait()
    incopies[0].wait()
    incopies[1].wait()
    pack_rows(range(H))
    for buf, order, edge in edges:
        for f in range(F):
            buf[EXTRA + f:EXTRA + f + 1, :] = x[f, order[2]:order[2] + 1, :]
        buf[EXTRA + F:EXTRA + F + 1, :] = coef[edge:edge + 1, :]
        buf[EXTRA + F + 1:EXTRA + F + 2, :] = air_warm[edge:edge + 1, :]

    total = jnp.int32(0)
    for dc, dt in around:
        total = total + there(dc, dt).astype(jnp.int32)
    pl.semaphore_wait(barrier, total)
    send(0)
    send(1)

    for l in range(H, L):
        xcopy(l).wait()
    incopies[2].wait()
    incopies[3].wait()
    lanes = iota((R, LANES), 1)
    mlane = iota((MR, LANES), 1)
    for buf, at, mat, near, second in ((CF, 0, 0, 0, 1), (CL, W - LANES, OW - LANES, LANES - 1, LANES - 2)):
        acc = jnp.zeros((R, LANES), jnp.float32)
        for k in range(F * L):
            f, l = divmod(k, L)
            tile = x[f, pl.ds(l * R, R), pl.ds(at, LANES)]
            acc = jnp.where(lanes == k, col_roll(tile, k - near), acc)
            acc = jnp.where(lanes == HALF + k, col_roll(tile, HALF + k - second), acc)
        buf[pl.ds(0, R), :] = acc
        macc = jnp.zeros((MR, LANES), jnp.float32)
        for k in range(MF + 1):
            tile = flows[pl.ds(k * MR, MR), pl.ds(mat, LANES)] if k < MF else warm[:, pl.ds(mat, LANES)]
            macc = jnp.where(mlane == k, col_roll(tile, k - near), macc)
        buf[pl.ds(R, MR), :] = macc
    for i in range(2, 8):
        send(i)
    pack_rows(range(H, L))
    for buf, row in ((OF, 0), (OL, MR - 1)):
        for k in range(MF):
            buf[k:k + 1, :] = flows[k * MR + row:k * MR + row + 1, :]
        buf[MF:MF + 1, :] = warm[row:row + 1, :]
    for i in range(8, len(plan)):
        send(i)
    for i in range(len(plan)):
        @pl.when(jnp.logical_not(there(-plan[i][0], -plan[i][1])))
        def _(i=i):
            dst = plan[i][3]
            dst[...] = jnp.zeros(dst.shape, jnp.float32)

    rowid = iota((R, W), 0)
    colid = iota((R, W), 1)

    def beside_rows(v, north, south):
        ids = rowid[0:v.shape[0], 0:v.shape[1]]
        return (jnp.where(ids == 0, north, row_roll(v, 1)),
                jnp.where(ids == v.shape[0] - 1, south, row_roll(v, -1)))

    def widen(v, west, east):
        return jnp.concatenate([west, v, east], axis=1)

    def beside_cols(v, west, east):
        wide = widen(v, west, east)
        return (col_roll(wide, 1)[:, LANES:LANES + v.shape[1]],
                col_roll(wide, -1)[:, LANES:LANES + v.shape[1]])

    def self_and_levels(src, f, l):
        v = src[f, rows_of(l), :]
        return v, src[f, rows_of(jnp.minimum(l + 1, L - 1)), :] + src[f, rows_of(jnp.maximum(l - 1, 0)), :]

    @pl.loop(0, L)
    def _(l):
        parts = []
        for f in range(F):
            v, both = self_and_levels(x, f, l)
            p, q = beside_rows(v, 0.0, 0.0)
            a = jnp.where(colid == 0, 0.0, col_roll(v, 1))
            b = jnp.where(colid == W - 1, 0.0, col_roll(v, -1))
            parts.append((v, p, q, a, b, both))
        new = update(*parts)
        for f in range(F):
            s1[f, rows_of(l), :] = new[f]

    def halo(D, f, deep, half):
        at = slot(f, half * H, deep)
        return D[at:at + H, :]

    def fix_rows(half):
        for D, fix, sign in ((RN, fixn, 0.5), (RS, fixs, -0.5)):
            e, n, h = (halo(D, f, 0, half) for f in range(F))
            for f, v in enumerate((e, n + sign * h, h + sign * n)):
                fix[f * L + half * H:f * L + half * H + H, :] = STEP * v

    def fix_cols():
        for C, fix, sign in ((CW, fixw, 0.5), (CE, fixe, -0.5)):
            mid = C[1, 0:R, :]
            v = jnp.where(lanes < L, mid + sign * col_roll(mid, -2 * L), mid)
            v = jnp.where(lanes >= 2 * L, mid + sign * col_roll(mid, 2 * L), v)
            fix[...] = STEP * v

    row8 = iota((8, W), 0)

    def add_fixes(lo, hi):
        west, east = fixw[...], fixe[...]

        @pl.loop(lo, hi)
        def _(l):
            for f in range(F):
                k = f * L + l
                top = pl.ds(pl.multiple_of(l * R, R), 8)
                low = pl.ds(pl.multiple_of(l * R + R - 8, 8), 8)
                s1[f, top, :] = s1[f, top, :] + jnp.where(row8 == 0, fixn[pl.ds(k, 1), :], 0.0)
                s1[f, low, :] = s1[f, low, :] + jnp.where(row8 == 7, fixs[pl.ds(k, 1), :], 0.0)
                at = rows_of(l)
                s1[f, at, first] = s1[f, at, first] + jnp.where(
                    lanes == 0, pltpu.roll(west, lax.rem(LANES - k, LANES), 1), 0.0)
                s1[f, at, last] = s1[f, at, last] + jnp.where(
                    lanes == LANES - 1, pltpu.roll(east, LANES - 1 - k, 1), 0.0)

    def side(C, own):
        mid = C[1, 0:R, :]
        tall = jnp.concatenate([C[0, 0:R, :], mid, C[2, 0:R, :]], axis=0)
        p, q = row_roll(tall, 1)[R:2 * R], row_roll(tall, -1)[R:2 * R]
        outer = col_roll(mid, -HALF)
        inner = own[0:R, :]
        lev = lanes % L
        up = jnp.where(lev == L - 1, mid, col_roll(mid, -1))
        down = jnp.where(lev == 0, mid, col_roll(mid, 1))
        return mid, p, q, outer, inner, up + down

    def side_step(mid, p, q, a, b, v):
        def moved(f):
            return tuple(col_roll(u, -f * L) for u in (mid, p, q, a, b, v))
        new = update(moved(0), moved(1), moved(2))
        acc = new[0]
        for f in range(1, F):
            acc = jnp.where(lanes >= f * L, col_roll(new[f], f * L), acc)
        return acc

    wide_lanes = iota((1, W + 2 * LANES), 1)
    in_cols = jnp.logical_and(jnp.logical_or(wide_lanes >= LANES, c > 0),
                              jnp.logical_or(wide_lanes < LANES + W, c < n_comp - 1))
    mids = slice(LANES, LANES + W)
    north_of = (True, 0, RF, t > 0, DNW, RN, DNE, s1n)
    south_of = (False, R - 1, RL, t < n_tile - 1, DSW, RS, DSE, s1s)

    def ring_rows(where_, halves):
        near, own_row, OWN, valid, DW, D, DE, ring = where_
        n = halves * H
        lev = iota((n, W + 2 * LANES), 0)
        tlev = iota((n, LANES), 0)
        tlane = iota((n, LANES), 1)

        def stacked(buf, f, deep):
            return jnp.concatenate([halo(buf, f, deep, i) for i in range(halves)], axis=0)

        parts, outers = [], []
        for f in range(F):
            k = f * L
            center = widen(stacked(D, f, 0), stacked(DW, f, 0), stacked(DE, f, 0))
            outer = widen(stacked(D, f, 1), stacked(DW, f, 1), stacked(DE, f, 1))
            west = jnp.where((tlev == 0) & (tlane == LANES - 1),
                             jnp.broadcast_to(CW[1, own_row:own_row + 1, k:k + 1], (n, LANES)), 0.0)
            east = jnp.where((tlev == 0) & (tlane == 0),
                             jnp.broadcast_to(CE[1, own_row:own_row + 1, k:k + 1], (n, LANES)), 0.0)
            inner = widen(stacked(OWN, f, 0), west, east)
            p, q = (outer, inner) if near else (inner, outer)
            both = (jnp.where(lev == n - 1, center, row_roll(center, -1))
                    + jnp.where(lev == 0, center, row_roll(center, 1)))
            parts.append((center, p, q, col_roll(center, 1), col_roll(center, -1), both))
            outers.append(outer)
        ok = jnp.logical_and(in_cols, valid)
        new = [jnp.where(ok, s, 0.0) for s in update(*parts)]
        for f in range(F):
            ring[f * L:f * L + n, :] = new[f][:, mids]
        return new, [p[0] for p in parts], outers

    def fluxes(e, n, h, co, wa):
        gain = co * jnp.sqrt(e * e + n * n + GUST)
        return gain * e, gain * n, gain * (wa - h)

    def edge_flux(where_):
        near, own_row, OWN, valid, DW, D, DE, ring = where_
        s_near, centers, outers = ring_rows(where_, 1)
        parts = []
        for f in range(F):
            at = slice(EXTRA + f, EXTRA + f + 1)
            third = widen(D[at, :], DW[at, :], DE[at, :])
            far = outers[f][0:1]
            p, q = (third, centers[f][0:1]) if near else (centers[f][0:1], third)
            parts.append((far, p, q, col_roll(far, 1), col_roll(far, -1), far + outers[f][1:2]))
        s_far = update(*parts)
        parts = []
        for f in range(F):
            v = s_near[f][0:1]
            inner = s1[f, pl.ds(own_row, 1), :]
            p, q = (s_far[f][:, mids], inner) if near else (inner, s_far[f][:, mids])
            parts.append((v[:, mids], p, q, col_roll(v, 1)[:, mids], col_roll(v, -1)[:, mids],
                          v[:, mids] + s_near[f][1:2, mids]))
        e, n, h = update(*parts)
        return fluxes(e, n, h, D[EXTRA + F:EXTRA + F + 1, :], D[EXTRA + F + 1:EXTRA + F + 2, :])

    def split(flux):
        high = [f.astype(jnp.bfloat16).astype(jnp.float32) for f in flux]
        return high + [f - g for f, g in zip(flux, high)] + [jnp.ones_like(flux[0]), jnp.zeros_like(flux[0])]

    def second(l):
        west, east = s1w[...], s1e[...]
        parts = []
        for f in range(F):
            k = f * L + l
            v, both = self_and_levels(s1, f, l)
            p, q = beside_rows(v, s1n[pl.ds(k, 1), :], s1s[pl.ds(k, 1), :])
            a, b = beside_cols(v, pltpu.roll(west, LANES - 1 - k, 1), pltpu.roll(east, lax.rem(LANES - k, LANES), 1))
            parts.append((v, p, q, a, b, both))
        new = update(*parts)
        for f in range(F):
            s2[f, rows_of(l), :] = new[f]
        ocopy(l).start()

    for i in range(len(plan)):
        if i not in LATE:
            receive(i)
    mid, p, q, a, b, v = side(CW, CF)
    s1w[...] = jnp.where(c > 0, side_step(mid, p, q, a, b, v), 0.0)
    mid, p, q, a, b, v = side(CE, CL)
    s1e[...] = jnp.where(c < n_comp - 1, side_step(mid, p, q, b, a, v), 0.0)
    fix_cols()
    fix_rows(0)
    add_fixes(0, H)
    north = split(edge_flux(north_of))
    south = split(edge_flux(south_of))

    @pl.loop(0, H - 1)
    def _(l):
        second(l)

    own = split(fluxes(s2[0, 0:R, :], s2[1, 0:R, :], s2[2, 0:R, :], coef[...], air_warm[...]))
    for j in range(CB):
        at = slice(j * LANES, (j + 1) * LANES)
        for i in range(8):
            fx[j, i:i + 1, :] = north[i][:, at]
            fx[pl.ds(CB + j, R, stride=CB), i, :] = own[i][:, at]
            fx[(R + 1) * CB + j, i:i + 1, :] = south[i][:, at]

    for copy_in in incopies[4:]:
        copy_in.wait()
    base = (t * R - 1) * CB
    for g in range(NOB):
        tiles = []
        for s in range(NOV):
            live = jnp.clip(count[0, g] - s, 0, 1).astype(jnp.float32)
            tiles.append(fx[jnp.clip(part[s, g] - base, 0, fx.shape[0] - 1)] * live)
        operand = jnp.concatenate(tiles, axis=1).astype(jnp.bfloat16)
        res[pl.ds(g * 8, 8), :] = jnp.dot(operand, weights[g], preferred_element_type=jnp.float32)

    cols = OW // LANES

    def gathered(i):
        return jnp.concatenate([res[pl.ds(q * 8 + i, MR, stride=cols * 8), :] for q in range(cols)], axis=1)

    below = gathered(2 * F)
    push = [(gathered(f) + gathered(F + f)) / below for f in range(F)]

    mask = water[...].astype(jnp.float32)
    ow, oe = CW[1, R:R + MR, :], CE[1, R:R + MR, :]

    def neighbours(k, v):
        p, q = beside_rows(v, ON[k:k + 1, :], OS[k:k + 1, :])
        a, b = beside_cols(v, col_roll(ow, LANES - 1 - k), col_roll(oe, -k))
        return p, q, a, b

    for l in range(ML):
        E = flows[l * MR:(l + 1) * MR, :]
        N = flows[(ML + l) * MR:(ML + l + 1) * MR, :]
        for which, own_v, turned in ((0, E, COR * N), (1, N, -COR * E)):
            k = which * ML + l
            p, q, a, b = neighbours(k, own_v)
            hi = which * ML + min(l + 1, ML - 1)
            lo = which * ML + max(l - 1, 0)
            both = flows[hi * MR:(hi + 1) * MR, :] + flows[lo * MR:(lo + 1) * MR, :]
            total = turned + ((p + q) + (a + b)) + 0.5 * both
            if l == 0:
                total = total + push[which]
            out_flows[k * MR:(k + 1) * MR, :] = mask * (STEP * total)
    T = warm[...]
    p, q, a, b = neighbours(2 * ML, T)
    carried = flows[0:MR, :] * (0.5 * (b - a)) + flows[ML * MR:(ML + 1) * MR, :] * (0.5 * (q - p))
    lap = (p + q) + (a + b) - 4.0 * T
    out_warm[...] = T + mask * STEP * (HEAT * push[2] - carried + DIFF * lap)
    outs = [pltpu.make_async_copy(out_flows, out_flows_hbm, osem.at[1]),
            pltpu.make_async_copy(out_warm, out_warm_hbm, osem.at[2])]
    for copy_out in outs:
        copy_out.start()

    for i in LATE:
        receive(i)
    fix_rows(1)
    add_fixes(H, L)
    ring_rows(north_of, 2)
    ring_rows(south_of, 2)

    @pl.loop(H - 1, L)
    def _(l):
        second(l)

    for i in range(len(plan)):
        @pl.when(there(plan[i][0], plan[i][1]))
        def _(i=i):
            copy(i).wait_send()
    for copy_out in outs:
        copy_out.wait()
    pltpu.make_async_copy(s2, out_hbm, osem.at[0]).wait()


def hand_on_kernel(x_hbm, flows_hbm, warm_hbm, out_hbm, out_flows_hbm, out_warm_hbm, x, flows, warm, isem, osem):
    pieces = isem.shape[0] - 2
    size = x.shape[1] // pieces

    def pair(i):
        if i < pieces:
            at = pl.ds(i * size, size)
            return ((x_hbm.at[:, at, :], x.at[:, at, :]), (x.at[:, at, :], out_hbm.at[:, at, :]))
        if i == pieces:
            return (flows_hbm, flows), (flows, out_flows_hbm)
        return (warm_hbm, warm), (warm, out_warm_hbm)

    order = [pieces, pieces + 1] + list(range(pieces))
    ins = {i: pltpu.make_async_copy(*pair(i)[0], isem.at[i]) for i in order}
    outs = {i: pltpu.make_async_copy(*pair(i)[1], osem.at[i]) for i in order}
    for i in order:
        ins[i].start()
    for i in order:
        ins[i].wait()
        outs[i].start()
    for i in order:
        outs[i].wait()


def shards(n_comp, n_tile, air, coef, air_warm, flows, warm, water, part, count, shares):
    F, L, R, W = air.shape
    MR, OW = warm.shape
    MF = flows.shape[0] * flows.shape[1]
    NOB, NOV = part.shape
    K = F * L
    dims = (F, L, R, W, MR, n_comp, n_tile)
    x = air.reshape(F, L * R, W)
    flows2 = flows.reshape(MF * MR, OW)
    rows = 2 * K + 8
    orows = -(-(MF + 1) // 8) * 8
    f32 = jnp.float32
    sds = jax.ShapeDtypeStruct
    hb = pl.BlockSpec(memory_space=pl.ANY)
    wshape = (NOB, NOV * LANES, LANES)
    halos = ([(rows, W)] * 2 + [(rows, LANES)] * 4 + [(3, R + MR, LANES)] * 2 + [(orows, OW)] * 2
             + [(R + MR, LANES)] * 2 + [(rows, W)] * 2 + [(orows, OW)] * 2)
    work = ([x.shape] * 2 + [(K, W)] * 4 + [(R, LANES)] * 4
            + [((R + 2) * (W // LANES), 8, LANES), (NOB * 8, LANES)])
    vf = [pltpu.VMEM(s, f32) for s in halos + work]
    nxt, new_flows, new_warm = pl.pallas_call(
        functools.partial(window_kernel, dims),
        out_shape=[sds(x.shape, f32), sds(flows2.shape, f32), sds(warm.shape, f32)],
        in_specs=[hb] * 9,
        out_specs=[hb] * 3,
        scratch_shapes=[
            pltpu.SMEM((NOV, NOB), jnp.int32), pltpu.SMEM((1, NOB), jnp.int32),
            pltpu.VMEM(x.shape, f32), pltpu.VMEM(coef.shape, f32), pltpu.VMEM(coef.shape, f32),
            pltpu.VMEM(flows2.shape, f32), pltpu.VMEM(warm.shape, f32), pltpu.VMEM(warm.shape, jnp.int32),
            pltpu.VMEM(wshape, jnp.bfloat16), pltpu.VMEM(flows2.shape, f32), pltpu.VMEM(warm.shape, f32)]
        + vf
        + [pltpu.SemaphoreType.DMA((L,)), pltpu.SemaphoreType.DMA((8,)), pltpu.SemaphoreType.DMA((3,)),
           pltpu.SemaphoreType.DMA((16,)), pltpu.SemaphoreType.DMA((16,))],
        compiler_params=pltpu.CompilerParams(collective_id=0, has_side_effects=True, vmem_limit_bytes=60 << 20),
        name="window",
    )(part.T, count.reshape(1, NOB), x, coef, air_warm, flows2, warm, water, shares.reshape(wshape))
    pieces = L // 2 if L % 2 == 0 else L
    nxt, new_flows, new_warm = pl.pallas_call(
        hand_on_kernel,
        out_shape=[sds(x.shape, f32), sds(flows2.shape, f32), sds(warm.shape, f32)],
        in_specs=[hb] * 3,
        out_specs=[hb] * 3,
        scratch_shapes=[pltpu.VMEM(x.shape, f32), pltpu.VMEM(flows2.shape, f32), pltpu.VMEM(warm.shape, f32),
                        pltpu.SemaphoreType.DMA((pieces + 2,)), pltpu.SemaphoreType.DMA((pieces + 2,))],
        compiler_params=pltpu.CompilerParams(vmem_limit_bytes=60 << 20),
        name="hand_on",
    )(nxt, new_flows, new_warm)
    return nxt.reshape(air.shape), new_flows.reshape(flows.shape), new_warm


def solution(mesh):
    placed = (
        P(None, None, "tile", "comp"),
        P("tile", "comp"),
        P("tile", "comp"),
        P(None, None, "tile", "comp"),
        P("tile", "comp"),
        P("tile", "comp"),
        P(("comp", "tile"), None),
        P(("comp", "tile")),
        P(("comp", "tile"), None, None, None),
    )
    return jax.shard_map(
        functools.partial(shards, mesh.shape["comp"], mesh.shape["tile"]),
        mesh=mesh,
        in_specs=placed,
        out_specs=(P(None, None, "tile", "comp"), P(None, None, "tile", "comp"), P("tile", "comp")),
        check_vma=False,
    )
```

```python
import functools
import jax
import jax.numpy as jnp
from jax import lax
from jax.experimental import pallas as pl
from jax.experimental.pallas import tpu as pltpu
from jax.sharding import PartitionSpec as P

MESH = pl.DeviceIdType.MESH
LANES = 128
HALF = 64

STEP = 0.2
COR = 0.3
VISC = 1.0
MIX = 0.5
GUST = 0.25
HEAT = 1.0
DIFF = 0.5
KEEP = round(1.0 - STEP * (4.0 * VISC + 2.0 * MIX), 12)
assert KEEP == 0.0


def col_roll(v, shift):
    return pltpu.roll(v, shift % v.shape[-1], v.ndim - 1)


def row_roll(v, shift):
    return pltpu.roll(v, shift % v.shape[-2], v.ndim - 2)


def iota(shape, axis):
    return lax.broadcasted_iota(jnp.int32, shape, axis)


def update(e, n, h):
    (ec, ep, en, el, er, ev), (nc, np_, nn, nl, nr, nv), (hc, hp, hn, hl, hr, hv) = e, n, h
    new_e = STEP * (COR * nc + ((ep + en) + (el + er)) + 0.5 * (hl - hr + ev))
    new_n = STEP * (-COR * ec + ((np_ + nn) + (nl + nr)) + 0.5 * (hp - hn + nv))
    new_h = STEP * (((hp + hn) + (hl + hr)) + 0.5 * ((el - er) + (np_ - nn) + hv))
    return new_e, new_n, new_h


def window_kernel(dims, part_hbm, count_hbm, x_hbm, coef_hbm, air_warm_hbm, flows_hbm, warm_hbm, water_hbm, weights_hbm,
                  out_hbm, out_flows_hbm, out_warm_hbm,
                  part, count, x, coef, air_warm, flows, warm, water, weights, out_flows, out_warm,
                  RN, RS, DNW, DNE, DSW, DSE, CW, CE, ON, OS, CF, CL, RF, RL, OF, OL,
                  s1, s2, s1n, s1s, fixn, fixs, s1w, s1e, fixw, fixe, fx, res,
                  xsem, insem, osem, ssem, rsem):
    F, L, R, W, MR, n_comp, n_tile = dims
    H = L // 2
    MF = flows.shape[0] // MR
    ML = MF // 2
    OW = flows.shape[1]
    NOB, NOV = weights.shape[0], weights.shape[1] // LANES
    CB = W // LANES
    FH = F * H
    EXTRA = 2 * FH
    EARLY = EXTRA + 8
    c = lax.axis_index("comp")
    t = lax.axis_index("tile")

    def there(dc, dt):
        oks = []
        if dc < 0:
            oks.append(c > 0)
        if dc > 0:
            oks.append(c < n_comp - 1)
        if dt < 0:
            oks.append(t > 0)
        if dt > 0:
            oks.append(t < n_tile - 1)
        ok = oks[0]
        for other in oks[1:]:
            ok = jnp.logical_and(ok, other)
        return ok

    around = [(dc, dt) for dc in (-1, 0, 1) for dt in (-1, 0, 1) if (dc, dt) != (0, 0)]
    barrier = pltpu.get_barrier_semaphore()
    for dc, dt in around:
        @pl.when(there(dc, dt))
        def _(dc=dc, dt=dt):
            pl.semaphore_signal(barrier, inc=1, device_id={"comp": c + dc, "tile": t + dt},
                                device_id_type=MESH)

    def rows_of(l):
        return pl.ds(pl.multiple_of(l * R, R), R)

    def xcopy(l):
        at = rows_of(l)
        return pltpu.make_async_copy(x_hbm.at[:, at, :], x.at[:, at, :], xsem.at[l])

    def ocopy(l):
        at = rows_of(l)
        return pltpu.make_async_copy(s2.at[:, at, :], out_hbm.at[:, at, :], osem.at[0])

    for l in range(L):
        xcopy(l).start()
    incopies = [pltpu.make_async_copy(src, dst, insem.at[i]) for i, (src, dst) in enumerate((
        (coef_hbm, coef), (air_warm_hbm, air_warm), (flows_hbm, flows), (warm_hbm, warm),
        (water_hbm, water), (part_hbm, part), (count_hbm, count), (weights_hbm, weights)))]
    for copy in incopies:
        copy.start()

    def slot(f, l, deep):
        return deep * FH + f * H + l if l < H else EARLY + deep * FH + f * H + l - H

    edges = ((RF, (0, 1, 2), 0), (RL, (R - 1, R - 2, R - 3), R - 1))

    def pack_rows(levels):
        for buf, order, _ in edges:
            for f in range(F):
                for l in levels:
                    for deep in range(2):
                        at = slot(f, l, deep)
                        buf[at:at + 1, :] = x[f, l * R + order[deep]:l * R + order[deep] + 1, :]

    first = pl.ds(0, LANES)
    last = pl.ds(W - LANES, LANES)
    early = pl.ds(0, EARLY)
    late = pl.ds(EARLY, 2 * FH)
    plan = [
        (0, -1, RF.at[early], RS.at[early]), (0, 1, RL.at[early], RN.at[early]),
        (-1, 0, CF, CE.at[1]), (1, 0, CL, CW.at[1]),
        (-1, -1, CF, CE.at[2]), (1, -1, CL, CW.at[2]),
        (-1, 1, CF, CE.at[0]), (1, 1, CL, CW.at[0]),
        (-1, -1, RF.at[:, first], DSE), (1, -1, RF.at[:, last], DSW),
        (-1, 1, RL.at[:, first], DNE), (1, 1, RL.at[:, last], DNW),
        (0, -1, OF, OS), (0, 1, OL, ON),
        (0, -1, RF.at[late], RS.at[late]), (0, 1, RL.at[late], RN.at[late]),
    ]
    LATE = (14, 15)

    def copy(i):
        dc, dt, src, dst = plan[i]
        return pltpu.make_async_remote_copy(
            src_ref=src, dst_ref=dst, send_sem=ssem.at[i], recv_sem=rsem.at[i],
            device_id={"comp": c + dc, "tile": t + dt}, device_id_type=MESH)

    def send(i):
        @pl.when(there(plan[i][0], plan[i][1]))
        def _():
            copy(i).start()

    def receive(i):
        @pl.when(there(-plan[i][0], -plan[i][1]))
        def _():
            copy(i).wait_recv()

    for l in range(H):
        xcopy(l).wait()
    incopies[0].wait()
    incopies[1].wait()
    pack_rows(range(H))
    for buf, order, edge in edges:
        for f in range(F):
            buf[EXTRA + f:EXTRA + f + 1, :] = x[f, order[2]:order[2] + 1, :]
        buf[EXTRA + F:EXTRA + F + 1, :] = coef[edge:edge + 1, :]
        buf[EXTRA + F + 1:EXTRA + F + 2, :] = air_warm[edge:edge + 1, :]

    total = jnp.int32(0)
    for dc, dt in around:
        total = total + there(dc, dt).astype(jnp.int32)
    pl.semaphore_wait(barrier, total)
    send(0)
    send(1)

    for l in range(H, L):
        xcopy(l).wait()
    incopies[2].wait()
    incopies[3].wait()
    lanes = iota((R, LANES), 1)
    mlane = iota((MR, LANES), 1)
    for buf, at, mat, near, second in ((CF, 0, 0, 0, 1), (CL, W - LANES, OW - LANES, LANES - 1, LANES - 2)):
        acc = jnp.zeros((R, LANES), jnp.float32)
        for k in range(F * L):
            f, l = divmod(k, L)
            tile = x[f, pl.ds(l * R, R), pl.ds(at, LANES)]
            acc = jnp.where(lanes == k, col_roll(tile, k - near), acc)
            acc = jnp.where(lanes == HALF + k, col_roll(tile, HALF + k - second), acc)
        buf[pl.ds(0, R), :] = acc
        macc = jnp.zeros((MR, LANES), jnp.float32)
        for k in range(MF + 1):
            tile = flows[pl.ds(k * MR, MR), pl.ds(mat, LANES)] if k < MF else warm[:, pl.ds(mat, LANES)]
            macc = jnp.where(mlane == k, col_roll(tile, k - near), macc)
        buf[pl.ds(R, MR), :] = macc
    for i in range(2, 8):
        send(i)
    pack_rows(range(H, L))
    for buf, row in ((OF, 0), (OL, MR - 1)):
        for k in range(MF):
            buf[k:k + 1, :] = flows[k * MR + row:k * MR + row + 1, :]
        buf[MF:MF + 1, :] = warm[row:row + 1, :]
    for i in range(8, len(plan)):
        send(i)
    for i in range(len(plan)):
        @pl.when(jnp.logical_not(there(-plan[i][0], -plan[i][1])))
        def _(i=i):
            dst = plan[i][3]
            dst[...] = jnp.zeros(dst.shape, jnp.float32)

    rowid = iota((R, W), 0)
    colid = iota((R, W), 1)

    def beside_rows(v, north, south):
        ids = rowid[0:v.shape[0], 0:v.shape[1]]
        return (jnp.where(ids == 0, north, row_roll(v, 1)),
                jnp.where(ids == v.shape[0] - 1, south, row_roll(v, -1)))

    def widen(v, west, east):
        return jnp.concatenate([west, v, east], axis=1)

    def beside_cols(v, west, east):
        wide = widen(v, west, east)
        return (col_roll(wide, 1)[:, LANES:LANES + v.shape[1]],
                col_roll(wide, -1)[:, LANES:LANES + v.shape[1]])

    def self_and_levels(src, f, l):
        v = src[f, rows_of(l), :]
        return v, src[f, rows_of(jnp.minimum(l + 1, L - 1)), :] + src[f, rows_of(jnp.maximum(l - 1, 0)), :]

    @pl.loop(0, L)
    def _(l):
        parts = []
        for f in range(F):
            v, both = self_and_levels(x, f, l)
            p, q = beside_rows(v, 0.0, 0.0)
            a = jnp.where(colid == 0, 0.0, col_roll(v, 1))
            b = jnp.where(colid == W - 1, 0.0, col_roll(v, -1))
            parts.append((v, p, q, a, b, both))
        new = update(*parts)
        for f in range(F):
            s1[f, rows_of(l), :] = new[f]

    def halo(D, f, deep, half):
        at = slot(f, half * H, deep)
        return D[at:at + H, :]

    def fix_rows(half):
        for D, fix, sign in ((RN, fixn, 0.5), (RS, fixs, -0.5)):
            e, n, h = (halo(D, f, 0, half) for f in range(F))
            for f, v in enumerate((e, n + sign * h, h + sign * n)):
                fix[f * L + half * H:f * L + half * H + H, :] = STEP * v

    def fix_cols():
        for C, fix, sign in ((CW, fixw, 0.5), (CE, fixe, -0.5)):
            mid = C[1, 0:R, :]
            v = jnp.where(lanes < L, mid + sign * col_roll(mid, -2 * L), mid)
            v = jnp.where(lanes >= 2 * L, mid + sign * col_roll(mid, 2 * L), v)
            fix[...] = STEP * v

    row8 = iota((8, W), 0)

    def add_fixes(lo, hi, rows):
        west, east = fixw[...], fixe[...]

        @pl.loop(lo, hi)
        def _(l):
            for f in range(F):
                k = f * L + l
                if rows:
                    top = pl.ds(pl.multiple_of(l * R, R), 8)
                    low = pl.ds(pl.multiple_of(l * R + R - 8, 8), 8)
                    s1[f, top, :] = s1[f, top, :] + jnp.where(row8 == 0, fixn[pl.ds(k, 1), :], 0.0)
                    s1[f, low, :] = s1[f, low, :] + jnp.where(row8 == 7, fixs[pl.ds(k, 1), :], 0.0)
                at = rows_of(l)
                s1[f, at, first] = s1[f, at, first] + jnp.where(
                    lanes == 0, pltpu.roll(west, lax.rem(LANES - k, LANES), 1), 0.0)
                s1[f, at, last] = s1[f, at, last] + jnp.where(
                    lanes == LANES - 1, pltpu.roll(east, LANES - 1 - k, 1), 0.0)

    def late_terms(ring, fix, near):
        lev = iota((L, W), 0)
        col = iota((L, W), 1)
        sign = 0.5 if near else -0.5
        d = [jnp.where(lev >= H, fix[f * L:f * L + L, :], 0.0) for f in range(F)]
        parts = []
        for f in range(F):
            r = jnp.where(lev >= H - 1, ring[f * L:f * L + L, :], 0.0)
            zero = jnp.zeros_like(r)
            p, q = (r, zero) if near else (zero, r)
            a = jnp.where(col == 0, 0.0, col_roll(d[f], 1))
            b = jnp.where(col == W - 1, 0.0, col_roll(d[f], -1))
            both = (jnp.where(lev == L - 1, d[f], row_roll(d[f], -1))
                    + jnp.where(lev == 0, d[f], row_roll(d[f], 1)))
            parts.append((d[f], p, q, a, b, both))
        new = update(*parts)
        inside = (d[0], d[1] + sign * d[2], d[2] + sign * d[1])
        for f in range(F):
            ring[f * L:f * L + L, :] = new[f]
            fix[f * L:f * L + L, :] = STEP * inside[f]

    def side(C, own):
        mid = C[1, 0:R, :]
        tall = jnp.concatenate([C[0, 0:R, :], mid, C[2, 0:R, :]], axis=0)
        p, q = row_roll(tall, 1)[R:2 * R], row_roll(tall, -1)[R:2 * R]
        outer = col_roll(mid, -HALF)
        inner = own[0:R, :]
        lev = lanes % L
        up = jnp.where(lev == L - 1, mid, col_roll(mid, -1))
        down = jnp.where(lev == 0, mid, col_roll(mid, 1))
        return mid, p, q, outer, inner, up + down

    def side_step(mid, p, q, a, b, v):
        def moved(f):
            return tuple(col_roll(u, -f * L) for u in (mid, p, q, a, b, v))
        new = update(moved(0), moved(1), moved(2))
        acc = new[0]
        for f in range(1, F):
            acc = jnp.where(lanes >= f * L, col_roll(new[f], f * L), acc)
        return acc

    wide_lanes = iota((1, W + 2 * LANES), 1)
    in_cols = jnp.logical_and(jnp.logical_or(wide_lanes >= LANES, c > 0),
                              jnp.logical_or(wide_lanes < LANES + W, c < n_comp - 1))
    mids = slice(LANES, LANES + W)
    north_of = (True, 0, RF, t > 0, DNW, RN, DNE, s1n)
    south_of = (False, R - 1, RL, t < n_tile - 1, DSW, RS, DSE, s1s)

    def ring_rows(where_, halves):
        near, own_row, OWN, valid, DW, D, DE, ring = where_
        n = halves * H
        lev = iota((n, W + 2 * LANES), 0)
        tlev = iota((n, LANES), 0)
        tlane = iota((n, LANES), 1)

        def stacked(buf, f, deep):
            return jnp.concatenate([halo(buf, f, deep, i) for i in range(halves)], axis=0)

        parts, outers = [], []
        for f in range(F):
            k = f * L
            center = widen(stacked(D, f, 0), stacked(DW, f, 0), stacked(DE, f, 0))
            outer = widen(stacked(D, f, 1), stacked(DW, f, 1), stacked(DE, f, 1))
            west = jnp.where((tlev == 0) & (tlane == LANES - 1),
                             jnp.broadcast_to(CW[1, own_row:own_row + 1, k:k + 1], (n, LANES)), 0.0)
            east = jnp.where((tlev == 0) & (tlane == 0),
                             jnp.broadcast_to(CE[1, own_row:own_row + 1, k:k + 1], (n, LANES)), 0.0)
            inner = widen(stacked(OWN, f, 0), west, east)
            p, q = (outer, inner) if near else (inner, outer)
            both = (jnp.where(lev == n - 1, center, row_roll(center, -1))
                    + jnp.where(lev == 0, center, row_roll(center, 1)))
            parts.append((center, p, q, col_roll(center, 1), col_roll(center, -1), both))
            outers.append(outer)
        ok = jnp.logical_and(in_cols, valid)
        new = [jnp.where(ok, s, 0.0) for s in update(*parts)]
        for f in range(F):
            ring[f * L:f * L + n, :] = new[f][:, mids]
        return new, [p[0] for p in parts], outers

    def fluxes(e, n, h, co, wa):
        gain = co * jnp.sqrt(e * e + n * n + GUST)
        return gain * e, gain * n, gain * (wa - h)

    def edge_flux(where_):
        near, own_row, OWN, valid, DW, D, DE, ring = where_
        s_near, centers, outers = ring_rows(where_, 1)
        parts = []
        for f in range(F):
            at = slice(EXTRA + f, EXTRA + f + 1)
            third = widen(D[at, :], DW[at, :], DE[at, :])
            far = outers[f][0:1]
            p, q = (third, centers[f][0:1]) if near else (centers[f][0:1], third)
            parts.append((far, p, q, col_roll(far, 1), col_roll(far, -1), far + outers[f][1:2]))
        s_far = update(*parts)
        parts = []
        for f in range(F):
            v = s_near[f][0:1]
            inner = s1[f, pl.ds(own_row, 1), :]
            p, q = (s_far[f][:, mids], inner) if near else (inner, s_far[f][:, mids])
            parts.append((v[:, mids], p, q, col_roll(v, 1)[:, mids], col_roll(v, -1)[:, mids],
                          v[:, mids] + s_near[f][1:2, mids]))
        e, n, h = update(*parts)
        return fluxes(e, n, h, D[EXTRA + F:EXTRA + F + 1, :], D[EXTRA + F + 1:EXTRA + F + 2, :])

    def split(flux):
        high = [f.astype(jnp.bfloat16).astype(jnp.float32) for f in flux]
        return high + [f - g for f, g in zip(flux, high)] + [jnp.ones_like(flux[0]), jnp.zeros_like(flux[0])]

    def second(l, ringed):
        west, east = s1w[...], s1e[...]
        parts = []
        for f in range(F):
            k = f * L + l
            v, both = self_and_levels(s1, f, l)
            p, q = beside_rows(v, s1n[pl.ds(k, 1), :] if ringed else 0.0, s1s[pl.ds(k, 1), :] if ringed else 0.0)
            a, b = beside_cols(v, pltpu.roll(west, LANES - 1 - k, 1), pltpu.roll(east, lax.rem(LANES - k, LANES), 1))
            parts.append((v, p, q, a, b, both))
        new = update(*parts)
        for f in range(F):
            s2[f, rows_of(l), :] = new[f]

    for i in range(len(plan)):
        if i not in LATE:
            receive(i)
    mid, p, q, a, b, v = side(CW, CF)
    s1w[...] = jnp.where(c > 0, side_step(mid, p, q, a, b, v), 0.0)
    mid, p, q, a, b, v = side(CE, CL)
    s1e[...] = jnp.where(c < n_comp - 1, side_step(mid, p, q, b, a, v), 0.0)
    fix_cols()
    fix_rows(0)
    add_fixes(0, H, True)
    add_fixes(H, L, False)
    north = split(edge_flux(north_of))
    south = split(edge_flux(south_of))

    @pl.loop(0, H - 1)
    def _(l):
        second(l, True)
        ocopy(l).start()

    own = split(fluxes(s2[0, 0:R, :], s2[1, 0:R, :], s2[2, 0:R, :], coef[...], air_warm[...]))
    for j in range(CB):
        at = slice(j * LANES, (j + 1) * LANES)
        for i in range(8):
            fx[j, i:i + 1, :] = north[i][:, at]
            fx[pl.ds(CB + j, R, stride=CB), i, :] = own[i][:, at]
            fx[(R + 1) * CB + j, i:i + 1, :] = south[i][:, at]

    for copy_in in incopies[4:]:
        copy_in.wait()
    base = (t * R - 1) * CB
    for g in range(NOB):
        tiles = []
        for s in range(NOV):
            live = jnp.clip(count[0, g] - s, 0, 1).astype(jnp.float32)
            tiles.append(fx[jnp.clip(part[s, g] - base, 0, fx.shape[0] - 1)] * live)
        operand = jnp.concatenate(tiles, axis=1).astype(jnp.bfloat16)
        res[pl.ds(g * 8, 8), :] = jnp.dot(operand, weights[g], preferred_element_type=jnp.float32)

    cols = OW // LANES

    def gathered(i):
        return jnp.concatenate([res[pl.ds(q * 8 + i, MR, stride=cols * 8), :] for q in range(cols)], axis=1)

    below = gathered(2 * F)
    push = [(gathered(f) + gathered(F + f)) / below for f in range(F)]

    mask = water[...].astype(jnp.float32)
    ow, oe = CW[1, R:R + MR, :], CE[1, R:R + MR, :]

    def neighbours(k, v):
        p, q = beside_rows(v, ON[k:k + 1, :], OS[k:k + 1, :])
        a, b = beside_cols(v, col_roll(ow, LANES - 1 - k), col_roll(oe, -k))
        return p, q, a, b

    for l in range(ML):
        E = flows[l * MR:(l + 1) * MR, :]
        N = flows[(ML + l) * MR:(ML + l + 1) * MR, :]
        for which, own_v, turned in ((0, E, COR * N), (1, N, -COR * E)):
            k = which * ML + l
            p, q, a, b = neighbours(k, own_v)
            hi = which * ML + min(l + 1, ML - 1)
            lo = which * ML + max(l - 1, 0)
            both = flows[hi * MR:(hi + 1) * MR, :] + flows[lo * MR:(lo + 1) * MR, :]
            total = turned + ((p + q) + (a + b)) + 0.5 * both
            if l == 0:
                total = total + push[which]
            out_flows[k * MR:(k + 1) * MR, :] = mask * (STEP * total)
    T = warm[...]
    p, q, a, b = neighbours(2 * ML, T)
    carried = flows[0:MR, :] * (0.5 * (b - a)) + flows[ML * MR:(ML + 1) * MR, :] * (0.5 * (q - p))
    lap = (p + q) + (a + b) - 4.0 * T
    out_warm[...] = T + mask * STEP * (HEAT * push[2] - carried + DIFF * lap)
    outs = [pltpu.make_async_copy(out_flows, out_flows_hbm, osem.at[1]),
            pltpu.make_async_copy(out_warm, out_warm_hbm, osem.at[2])]
    for copy_out in outs:
        copy_out.start()

    @pl.loop(H - 1, L)
    def _(l):
        second(l, False)

    for i in LATE:
        receive(i)
    fix_rows(1)
    ring_rows(north_of, 2)
    ring_rows(south_of, 2)
    late_terms(s1n, fixn, True)
    late_terms(s1s, fixs, False)

    @pl.loop(H - 1, L)
    def _(l):
        for f in range(F):
            k = f * L + l
            top = pl.ds(pl.multiple_of(l * R, R), 8)
            low = pl.ds(pl.multiple_of(l * R + R - 8, 8), 8)
            s2[f, top, :] = s2[f, top, :] + jnp.where(
                row8 == 0, s1n[pl.ds(k, 1), :], jnp.where(row8 == 1, fixn[pl.ds(k, 1), :], 0.0))
            s2[f, low, :] = s2[f, low, :] + jnp.where(
                row8 == 7, s1s[pl.ds(k, 1), :], jnp.where(row8 == 6, fixs[pl.ds(k, 1), :], 0.0))
        ocopy(l).start()

    for i in range(len(plan)):
        @pl.when(there(plan[i][0], plan[i][1]))
        def _(i=i):
            copy(i).wait_send()
    for copy_out in outs:
        copy_out.wait()
    pltpu.make_async_copy(s2, out_hbm, osem.at[0]).wait()


def hand_on_kernel(x_hbm, flows_hbm, warm_hbm, out_hbm, out_flows_hbm, out_warm_hbm, x, flows, warm, isem, osem):
    pieces = isem.shape[0] - 2
    size = x.shape[1] // pieces

    def pair(i):
        if i < pieces:
            at = pl.ds(i * size, size)
            return ((x_hbm.at[:, at, :], x.at[:, at, :]), (x.at[:, at, :], out_hbm.at[:, at, :]))
        if i == pieces:
            return (flows_hbm, flows), (flows, out_flows_hbm)
        return (warm_hbm, warm), (warm, out_warm_hbm)

    order = [pieces, pieces + 1] + list(range(pieces))
    ins = {i: pltpu.make_async_copy(*pair(i)[0], isem.at[i]) for i in order}
    outs = {i: pltpu.make_async_copy(*pair(i)[1], osem.at[i]) for i in order}
    for i in order:
        ins[i].start()
    for i in order:
        ins[i].wait()
        outs[i].start()
    for i in order:
        outs[i].wait()


def shards(n_comp, n_tile, air, coef, air_warm, flows, warm, water, part, count, shares):
    F, L, R, W = air.shape
    MR, OW = warm.shape
    MF = flows.shape[0] * flows.shape[1]
    NOB, NOV = part.shape
    K = F * L
    dims = (F, L, R, W, MR, n_comp, n_tile)
    x = air.reshape(F, L * R, W)
    flows2 = flows.reshape(MF * MR, OW)
    rows = 2 * K + 8
    orows = -(-(MF + 1) // 8) * 8
    f32 = jnp.float32
    sds = jax.ShapeDtypeStruct
    hb = pl.BlockSpec(memory_space=pl.ANY)
    wshape = (NOB, NOV * LANES, LANES)
    halos = ([(rows, W)] * 2 + [(rows, LANES)] * 4 + [(3, R + MR, LANES)] * 2 + [(orows, OW)] * 2
             + [(R + MR, LANES)] * 2 + [(rows, W)] * 2 + [(orows, OW)] * 2)
    work = ([x.shape] * 2 + [(K, W)] * 4 + [(R, LANES)] * 4
            + [((R + 2) * (W // LANES), 8, LANES), (NOB * 8, LANES)])
    vf = [pltpu.VMEM(s, f32) for s in halos + work]
    nxt, new_flows, new_warm = pl.pallas_call(
        functools.partial(window_kernel, dims),
        out_shape=[sds(x.shape, f32), sds(flows2.shape, f32), sds(warm.shape, f32)],
        in_specs=[hb] * 9,
        out_specs=[hb] * 3,
        scratch_shapes=[
            pltpu.SMEM((NOV, NOB), jnp.int32), pltpu.SMEM((1, NOB), jnp.int32),
            pltpu.VMEM(x.shape, f32), pltpu.VMEM(coef.shape, f32), pltpu.VMEM(coef.shape, f32),
            pltpu.VMEM(flows2.shape, f32), pltpu.VMEM(warm.shape, f32), pltpu.VMEM(warm.shape, jnp.int32),
            pltpu.VMEM(wshape, jnp.bfloat16), pltpu.VMEM(flows2.shape, f32), pltpu.VMEM(warm.shape, f32)]
        + vf
        + [pltpu.SemaphoreType.DMA((L,)), pltpu.SemaphoreType.DMA((8,)), pltpu.SemaphoreType.DMA((3,)),
           pltpu.SemaphoreType.DMA((16,)), pltpu.SemaphoreType.DMA((16,))],
        compiler_params=pltpu.CompilerParams(collective_id=0, has_side_effects=True, vmem_limit_bytes=60 << 20),
        name="window",
    )(part.T, count.reshape(1, NOB), x, coef, air_warm, flows2, warm, water, shares.reshape(wshape))
    pieces = L // 2 if L % 2 == 0 else L
    nxt, new_flows, new_warm = pl.pallas_call(
        hand_on_kernel,
        out_shape=[sds(x.shape, f32), sds(flows2.shape, f32), sds(warm.shape, f32)],
        in_specs=[hb] * 3,
        out_specs=[hb] * 3,
        scratch_shapes=[pltpu.VMEM(x.shape, f32), pltpu.VMEM(flows2.shape, f32), pltpu.VMEM(warm.shape, f32),
                        pltpu.SemaphoreType.DMA((pieces + 2,)), pltpu.SemaphoreType.DMA((pieces + 2,))],
        compiler_params=pltpu.CompilerParams(vmem_limit_bytes=60 << 20),
        name="hand_on",
    )(nxt, new_flows, new_warm)
    return nxt.reshape(air.shape), new_flows.reshape(flows.shape), new_warm


def solution(mesh):
    placed = (
        P(None, None, "tile", "comp"),
        P("tile", "comp"),
        P("tile", "comp"),
        P(None, None, "tile", "comp"),
        P("tile", "comp"),
        P("tile", "comp"),
        P(("comp", "tile"), None),
        P(("comp", "tile")),
        P(("comp", "tile"), None, None, None),
    )
    return jax.shard_map(
        functools.partial(shards, mesh.shape["comp"], mesh.shape["tile"]),
        mesh=mesh,
        in_specs=placed,
        out_specs=(P(None, None, "tile", "comp"), P(None, None, "tile", "comp"), P("tile", "comp")),
        check_vma=False,
    )
```
